32 devices in a mesh: pts: 8 (over y, x, core), lst: 4 (over z).
Axes of the slice: x: 2, y: 2, z: 4, core: 2. Of those that a mesh axis runs over, the one named last changes fastest.
Arguments:
- tower_out: bfloat16 [16384, 1024], P('pts', 'lst'), may hold values from -6 to 6
- projection: bfloat16 [1024, 256], P('lst'), may hold values from -1 to 1
- centroids: bfloat16 [16384, 256], P('lst'), may hold values from -6 to 6
Outputs:
- new_centroids: float32 [16384, 256], P(('lst', 'pts'))
- row_log: float32 [16384], P('pts')
The draws below stay inside these ranges and needn't reach their ends.
All inputs are finite; a program needn't handle non-finite values.
Results may differ from the reference program's by a relative error of at most 0.0045.
Values may be sent and summed in bfloat16 or wider, within the bound.
A program may use at most 64 MiB of HBM per device.

```python
import math
import jax
import jax.numpy as jnp
from jax import lax

DIN = 1024
DP = 256
KC = 16384
ITERS = 3
NPTS = 16384


strength = 0.35


planted = 1.0


def plus_minus(seeded, total_count):
    return (jax.random.randint(seeded, (total_count,), 0, 2) * 2 - 1).astype(jnp.float32)


def tower_axis(key):
    return plus_minus(jax.random.fold_in(jax.random.fold_in(key, 101), 1), DIN)


def list_axis(key):
    return plus_minus(jax.random.fold_in(jax.random.fold_in(key, 101), 2), DP)


def group_signs(seeded, total_count, lowest, highest):
    border = jax.random.randint(seeded, (), lowest, highest)
    return jnp.where(jnp.arange(total_count) < border, 1.0, -1.0).astype(jnp.float32)


def draw_tower_out(key, part):
    tower_dir = tower_axis(key)
    point_sign = group_signs(jax.random.fold_in(key, 12), NPTS, 65 * NPTS // 100, 80 * NPTS // 100 + 1)
    jitter = jnp.clip(jax.random.normal(jax.random.fold_in(key, 11), (NPTS, DIN), jnp.float32), -5.5, 5.5)
    values = jitter + strength * point_sign[:, None] * tower_dir[None, :]
    return values.astype(jnp.bfloat16)


def draw_projection(key, part):
    tower_dir = tower_axis(key)
    list_dir = list_axis(key)
    dense = jnp.clip(jax.random.normal(jax.random.fold_in(key, 21), (DIN, DP), jnp.float32), -6.0, 6.0)
    values = dense * (1.0 / math.sqrt(DIN)) + planted / DIN * tower_dir[:, None] * list_dir[None, :]
    return values.astype(jnp.bfloat16)


def draw_centroids(key, part):
    list_dir = list_axis(key)
    list_sign = group_signs(jax.random.fold_in(key, 32), KC, 20 * KC // 100, 35 * KC // 100 + 1)
    jitter = jnp.clip(jax.random.normal(jax.random.fold_in(key, 31), (KC, DP), jnp.float32), -5.5, 5.5)
    values = jitter + strength * list_sign[:, None] * list_dir[None, :]
    return values.astype(jnp.bfloat16)


def setup_inputs(seed: int = 0) -> dict:
    key_list = jax.random.split(jax.random.key(seed), 4)
    tower_out = draw_tower_out(jax.random.fold_in(key_list[3], 71), 0)
    projection = draw_projection(jax.random.fold_in(key_list[3], 71), 0)
    centroids = draw_centroids(jax.random.fold_in(key_list[3], 71), 0)
    return dict(tower_out=tower_out, projection=projection, centroids=centroids)


temper = 0.05

def rms_norm(values):
    return values * lax.rsqrt(lax.optimization_barrier(jnp.mean(values * values, axis=-1, keepdims=True)) + 1e-06)

def energy(zblock, unit_lists):
    scores = lax.dot_general(zblock, unit_lists, (((1,), (1,)), ((), ())), preferred_element_type=jnp.float32)
    return jnp.exp(scores / (DP * temper) - 1.0 / temper)

def reference(tower_out, projection, centroids):
    hidden = jnp.dot(tower_out, projection, preferred_element_type=jnp.float32)
    normed = rms_norm(hidden).astype(jnp.bfloat16)
    unit_lists = rms_norm(centroids.astype(jnp.float32)).astype(jnp.bfloat16)
    block_rows = min(512, NPTS)
    block_count = NPTS // block_rows
    blocks = normed.reshape(block_count, block_rows, DP)
    balance = NPTS / KC
    row_scale = jnp.ones((NPTS,), jnp.float32)
    col_scale = jnp.ones((KC,), jnp.float32)
    for sweep in range(ITERS):

        def column_step(running, inputs):
            zblock, scale_blk = inputs
            return (running + lax.optimization_barrier(jnp.sum(energy(zblock, unit_lists) * scale_blk[:, None], axis=0)), None)
        column_sum = lax.scan(column_step, jnp.zeros((KC,), jnp.float32), (blocks, row_scale.reshape(block_count, block_rows)))[0]
        col_scale = balance / column_sum

        def row_step(zblock, scales=col_scale):
            return lax.optimization_barrier(jnp.sum(energy(zblock, unit_lists) * scales[None, :], axis=1))
        row_sum = lax.map(row_step, blocks).reshape(NPTS)
        row_scale = 1.0 / row_sum

    def update_step(running, inputs):
        zblock, scale_blk = inputs
        weights = (scale_blk[:, None] * energy(zblock, unit_lists) * col_scale[None, :]).astype(jnp.bfloat16)
        sums_part = lax.dot_general(weights, zblock, (((0,), (0,)), ((), ())), preferred_element_type=jnp.float32)
        return (running + sums_part, None)
    list_sums = lax.scan(update_step, jnp.zeros((KC, DP), jnp.float32), (blocks, row_scale.reshape(block_count, block_rows)))[0]
    return (rms_norm(list_sums), jnp.log(row_scale))
```

```python
import functools
import math
from types import SimpleNamespace

import jax
import jax.numpy as jnp
from jax import lax
from jax.experimental import pallas as pl
from jax.experimental.pallas import tpu as pltpu
from jax.sharding import PartitionSpec as P

ITERS = 3
temper = 0.05
LANES = 128
MESH = pl.DeviceIdType.MESH
F32 = jnp.float32
BF16 = jnp.bfloat16


def rms_norm(values):
    return values * lax.rsqrt(jnp.mean(values * values, axis=-1, keepdims=True) + 1e-06)


def column_of(row, rows):
    return jnp.broadcast_to(row, (rows, LANES)).T


def halved(values, rows):
    while values.shape[0] > rows:
        n = values.shape[0] // 2
        values = values[:n] + values[n:]
    return values


def added(terms):
    while len(terms) > 1:
        rest = terms[len(terms) // 2 * 2 :]
        terms = [terms[i] + terms[i + 1] for i in range(0, len(terms) - 1, 2)] + rest
    return terms[0]


def block(start, size):
    return pl.ds(pl.multiple_of(start * size, size), size)


def energy_block(s, gain, rows, cols, points):
    scores = lax.dot_general(
        s.unit[rows, :], points, (((1,), (1,)), ((), ())), preferred_element_type=F32
    )
    values = jnp.exp2(scores * gain)
    s.energy[rows, cols] = values.astype(BF16)
    width = values.shape[1] // LANES
    s.lane_sums[rows, :] += added([values[:, m * LANES : (m + 1) * LANES] for m in range(width)])


def unit_lists(s):
    lists = s.unit.shape[0]
    rows_each = min(256, lists)

    @pl.loop(0, lists // rows_each)
    def _(b):
        rows = block(b, rows_each)
        s.unit[rows, :] = rms_norm(s.unit[rows, :].astype(F32)).astype(BF16)
        s.lane_sums[rows, :] = jnp.zeros((rows_each, LANES), F32)


def line_gather(s, lst, gain, loads, arrive):
    points = s.tower.shape[0]
    lists = s.unit.shape[0]
    half = points // 2
    steps = half // LANES
    near = lst // 2
    far = 1 - near
    inner = (lst == 1) | (lst == 2)
    outer = jnp.logical_not(inner)
    inner_of_mine = 1 + near
    outer_of_mine = 3 * near
    other_inner = 2 - near

    def remote(src, dst, send_sem, recv_sem, target):
        return pltpu.make_async_remote_copy(
            src_ref=src,
            dst_ref=dst,
            send_sem=send_sem,
            recv_sem=recv_sem,
            device_id={"lst": target},
            device_id_type=MESH,
        )

    def feed(h, t):
        return remote(s.part.at[h, t], s.fed.at[h, t], s.f_send.at[h, t], s.f_recv.at[h, t], inner_of_mine)

    def cross(t):
        return remote(s.part.at[far, t], s.crossed.at[t], s.x_send.at[t], s.x_recv.at[t], other_inner)

    def back(u, h):
        return remote(
            s.normed.at[u, h], s.normed.at[u, h], s.b_send.at[u, h], s.n_recv.at[u, h], outer_of_mine
        )

    def across(u):
        return remote(
            s.normed.at[u, near], s.normed.at[u, near], s.a_send.at[u], s.n_recv.at[u, near], other_inner
        )

    def arrived(u, h):
        return remote(
            s.normed.at[u, h], s.normed.at[u, h], s.b_send.at[u, h], s.n_recv.at[u, h], other_inner
        )

    loads["proj"].wait()
    loads["tower"].wait()
    arrive()

    @pl.loop(0, steps)
    def _(t):
        for h in (far, near):
            values = jnp.dot(
                s.tower[block(h * steps + t, LANES), :], s.proj[...], preferred_element_type=F32
            )

            @pl.when(outer)
            def _(h=h, values=values):
                s.part[h, t] = values.astype(BF16)
                feed(h, t).start()

            @pl.when(inner)
            def _(h=h, values=values):
                s.own[h, t] = values

    loads["cent"].wait()
    unit_lists(s)
    e_rows = min(2048, lists)

    @pl.loop(0, steps + 2)
    def _(t):
        @pl.when(inner & (t < steps))
        def _():
            feed(far, t).wait_recv()
            s.part[far, t] = (s.own[far, t] + s.fed[far, t].astype(F32)).astype(BF16)
            cross(t).start()

        @pl.when(inner & (t >= 1) & (t <= steps))
        def _():
            u = t - 1
            feed(near, u).wait_recv()
            cross(u).wait_recv()
            hidden = s.own[near, u] + s.fed[near, u].astype(F32) + s.crossed[u].astype(F32)
            s.normed[u, near] = rms_norm(hidden).astype(BF16)
            back(u, near).start()
            across(u).start()

        @pl.when(t >= 2)
        def _():
            u = t - 2

            @pl.when(inner)
            def _():
                arrived(u, far).wait_recv()
                back(u, far).start()

            @pl.when(outer)
            def _():
                arrived(u, near).wait_recv()
                arrived(u, far).wait_recv()

            @pl.loop(0, lists // e_rows)
            def _(b):
                rows = block(b, e_rows)
                pair = s.normed[u].reshape(2 * LANES, s.normed.shape[-1])
                energy_block(s, gain, rows, block(u, 2 * LANES), pair)

    def settle():
        @pl.loop(0, steps)
        def _(t):
            @pl.when(outer)
            def _():
                feed(far, t).wait_send()
                feed(near, t).wait_send()

            @pl.when(inner)
            def _():
                cross(t).wait_send()
                back(t, near).wait_send()
                back(t, far).wait_send()
                across(t).wait_send()

    def points_of(m):
        return s.normed[m // 2, m % 2]

    return settle, points_of, [h * steps + u for u in range(steps) for h in range(2)]


def line_scratch(points, lists, feats, dp):
    half = points // 2
    steps = half // LANES
    sem = pltpu.SemaphoreType.DMA
    return dict(
        own=pltpu.VMEM((2, steps, LANES, dp), F32),
        part=pltpu.VMEM((2, steps, LANES, dp), BF16),
        fed=pltpu.VMEM((2, steps, LANES, dp), BF16),
        crossed=pltpu.VMEM((steps, LANES, dp), BF16),
        normed=pltpu.VMEM((steps, 2, LANES, dp), BF16),
        f_send=sem((2, steps)),
        f_recv=sem((2, steps)),
        x_send=sem((steps,)),
        x_recv=sem((steps,)),
        b_send=sem((steps, 2)),
        a_send=sem((steps,)),
        n_recv=sem((steps, 2)),
    )


def any_gather(s, nlst, npts, lst, pts, send, chunks, gain, loads, arrive):
    points = s.tower.shape[0]
    lists = s.unit.shape[0]
    share = points // nlst
    feats = s.proj.shape[0]
    loads["proj"].wait()
    loads["tower"].wait()
    arrive()
    piece = feats // npts
    sliced = piece % 16 == 0
    piece_rows = block(pts, piece) if sliced else pl.ds(0, feats)
    p_copies = [
        send(
            s.proj.at[piece_rows],
            s.pfull.at[d, piece_rows],
            s.p_send.at[d],
            s.p_recv.at[d],
            "lst",
            (lst + d) % nlst,
        )
        for d in range(1, nlst)
    ]
    chunk = share // chunks
    t_copies = []
    for c in range(chunks):
        for d in range(1, nlst):
            z = (lst + d) % nlst
            t_copies.append(
                send(
                    s.tower.at[block(z * chunks + c, chunk)],
                    s.full.at[c, d],
                    s.t_send.at[c, d],
                    s.t_recv.at[c, d],
                    "lst",
                    z,
                )
            )
    loads["cent"].wait()
    unit_lists(s)

    for copy in p_copies:
        copy.wait_recv()
    if sliced:
        q_copies = [
            send(
                s.pfull.at[pl.ds(1, nlst - 1), piece_rows],
                s.pfull.at[pl.ds(1, nlst - 1), piece_rows],
                s.q_send.at[d],
                s.q_recv.at[d],
                "pts",
                (pts + d) % npts,
            )
            for d in range(1, npts)
        ]
        for copy in q_copies:
            copy.wait_recv()

    def hop(c, origin, left):
        side = 0 if left else 1
        return pltpu.make_async_remote_copy(
            src_ref=s.normed.at[c, origin],
            dst_ref=s.normed.at[c, origin],
            send_sem=s.n_send.at[side, c, origin],
            recv_sem=s.n_recv.at[c, origin],
            device_id={"lst": lst - 1 if left else lst + 1},
            device_id_type=MESH,
        )

    has_left = lst > 0
    has_right = lst < nlst - 1
    for c in range(chunks):
        hidden = jnp.dot(
            s.tower[block(lst * chunks + c, chunk), :], s.proj[...], preferred_element_type=F32
        )
        for d in range(1, nlst):
            t_copies[c * (nlst - 1) + d - 1].wait_recv()
            hidden += jnp.dot(s.full[c, d], s.pfull[d], preferred_element_type=F32)
        s.normed[c, lst] = rms_norm(hidden).astype(BF16)

        @pl.when(has_left)
        def _(c=c):
            hop(c, lst, True).start()

        @pl.when(has_right)
        def _(c=c):
            hop(c, lst, False).start()

    e_rows = min(1024, lists)
    step = min(256, chunk)
    per_share = share // step
    per_chunk = chunk // step

    def energy_of(c, origin):
        @pl.loop(0, lists // e_rows)
        def _(b):
            rows = block(b, e_rows)
            for k in range(per_chunk):
                cols = block(origin * per_share + c * per_chunk + k, step)
                energy_block(s, gain, rows, cols, s.normed[c, origin, k * step : (k + 1) * step, :])

    paired = jnp.minimum(lst, nlst - 1 - lst)
    for n in range(nlst):
        close = (n + 1) // 2
        away = n - paired
        in_pairs = lst - close if n % 2 else lst + close
        beyond = jnp.where(has_right & (lst < nlst - 1 - lst), lst + away, lst - away)
        origin = jnp.where(n <= 2 * paired, in_pairs, beyond) if n else lst
        for c in range(chunks):
            if n:
                hop(c, origin, True).wait_recv()

                @pl.when((origin < lst) & has_right)
                def _(c=c, origin=origin):
                    hop(c, origin, False).start()

                @pl.when((origin > lst) & has_left)
                def _(c=c, origin=origin):
                    hop(c, origin, True).start()

            energy_of(c, origin)

    def settle():
        for z in range(nlst):
            for c in range(chunks):

                @pl.when((z <= lst) & has_right)
                def _(c=c, z=z):
                    hop(c, z, False).wait_send()

                @pl.when((z >= lst) & has_left)
                def _(c=c, z=z):
                    hop(c, z, True).wait_send()

    def points_of(m):
        d, k = divmod(m * LANES, share)
        c, k = divmod(k, chunk)
        return s.normed[c, d, k : k + LANES, :]

    return settle, points_of, list(range(points // LANES))


def any_scratch(points, lists, feats, dp, npts, nlst, chunks):
    chunk = points // nlst // chunks
    sem = pltpu.SemaphoreType.DMA
    return dict(
        full=pltpu.VMEM((chunks, nlst, chunk, feats), BF16),
        pfull=pltpu.VMEM((nlst, feats, dp), BF16),
        normed=pltpu.VMEM((chunks, nlst, chunk, dp), BF16),
        t_send=sem((chunks, nlst)),
        t_recv=sem((chunks, nlst)),
        p_send=sem((nlst,)),
        p_recv=sem((nlst,)),
        q_send=sem((npts,)),
        q_recv=sem((npts,)),
        n_send=sem((2, chunks, nlst)),
        n_recv=sem((chunks, nlst)),
    )


def kernel(npts, nlst, chunks, names, tower, proj, cent, out, row_log, *scratch):
    s = SimpleNamespace(**dict(zip(names, scratch)))
    pts = lax.axis_index("pts")
    lst = lax.axis_index("lst")
    lists, dp = s.unit.shape
    points = s.tower.shape[0]
    own = lists // npts
    chips = npts // 2
    core = pts % 2
    chip = pts // 2
    balance = (points * npts) / (lists * nlst)
    list_blocks = lists // LANES
    point_blocks = points // LANES

    loads = {
        "proj": pltpu.make_async_copy(proj, s.proj, s.load.at[0]),
        "tower": pltpu.make_async_copy(tower, s.tower, s.load.at[1]),
        "cent": pltpu.make_async_copy(cent, s.unit, s.load.at[2]),
    }
    for copy in loads.values():
        copy.start()

    barrier = pltpu.get_barrier_semaphore()
    for d in range(1, nlst):
        pl.semaphore_signal(
            barrier, inc=1, device_id={"lst": (lst + d) % nlst}, device_id_type=MESH
        )
    for d in range(1, npts):
        pl.semaphore_signal(
            barrier, inc=1, device_id={"pts": (pts + d) % npts}, device_id_type=MESH
        )

    def arrive():
        pl.semaphore_wait(barrier, nlst + npts - 2)

    pending = []

    def send(src, dst, send_sem, recv_sem, axis, target):
        copy = pltpu.make_async_remote_copy(
            src_ref=src,
            dst_ref=dst,
            send_sem=send_sem,
            recv_sem=recv_sem,
            device_id={axis: target},
            device_id_type=MESH,
        )
        copy.start()
        pending.append(copy)
        return copy

    gain = 1.0 / (math.log(2.0) * dp * temper)
    if in_line(points, nlst):
        settle, points_of, place = line_gather(s, lst, gain, loads, arrive)
    else:
        settle, points_of, place = any_gather(
            s, nlst, npts, lst, pts, send, chunks, gain, loads, arrive
        )

    def lane_dense(sums):
        return jnp.sum(sums.T, axis=0, keepdims=True)

    row_scale = None
    for sweep in range(ITERS):
        if sweep == 0:

            @pl.loop(0, list_blocks, unroll=4)
            def _(b):
                s.dense[pl.ds(b, 1), :] = lane_dense(s.lane_sums[block(b, LANES), :])
        else:
            wide = [
                jnp.broadcast_to(row_scale[m : m + 1, :], (16, LANES)).astype(BF16)
                for m in range(point_blocks)
            ]

            @pl.loop(0, list_blocks, unroll=4)
            def _(b, wide=wide):
                groups = []
                for q in range(LANES // 16):
                    rows = block(b * (LANES // 16) + q, 16)
                    groups.append(
                        added(
                            [
                                s.energy[rows, m * LANES : (m + 1) * LANES] * wide[m]
                                for m in range(point_blocks)
                            ]
                        )
                    )
                s.dense[pl.ds(b, 1), :] = lane_dense(jnp.concatenate(groups, axis=0).astype(F32))

        s.col_sums[sweep, 0] = s.dense[...].astype(BF16)
        copies = [
            send(
                s.col_sums.at[sweep, 0],
                s.col_sums.at[sweep, d],
                s.c_send.at[sweep, d],
                s.c_recv.at[sweep, d],
                "pts",
                (pts + d) % npts,
            )
            for d in range(1, npts)
        ]
        for copy in copies:
            copy.wait_recv()
        total = added([s.col_sums[sweep, d].astype(F32) for d in range(npts)])
        s.dense[...] = balance / total

        def row_step(b, acc):
            rows = block(b, LANES)
            wide = column_of(s.dense[pl.ds(b, 1), :], LANES).astype(BF16)
            parts = []
            for m in range(point_blocks):
                term = halved(s.energy[rows, m * LANES : (m + 1) * LANES] * wide, 16).astype(F32)
                parts.append(acc[m] + halved(term, 8))
            return tuple(parts)

        acc = lax.fori_loop(
            0,
            list_blocks,
            row_step,
            tuple(jnp.zeros((8, LANES), F32) for _ in range(point_blocks)),
            unroll=4,
        )
        s.row_sums[sweep, 0] = jnp.concatenate(
            [jnp.sum(part, axis=0, keepdims=True) for part in acc], axis=0
        )
        copies = [
            send(
                s.row_sums.at[sweep, 0],
                s.row_sums.at[sweep, d],
                s.r_send.at[sweep, d],
                s.r_recv.at[sweep, d],
                "lst",
                (lst + d) % nlst,
            )
            for d in range(1, nlst)
        ]
        for copy in copies:
            copy.wait_recv()
        row_scale = 1.0 / added([s.row_sums[sweep, d] for d in range(nlst)])
    logs = jnp.log(row_scale)
    for m in range(point_blocks):
        row_log[place[m] : place[m] + 1, :] = logs[m : m + 1, :]

    for m in range(point_blocks):
        wide = column_of(row_scale[m : m + 1, :], LANES)
        values = points_of(m).astype(F32)
        for h in range(dp // LANES):
            lanes = slice(h * LANES, (h + 1) * LANES)
            s.scaled[m * LANES : (m + 1) * LANES, lanes] = (values[:, lanes] * wide).astype(BF16)

    tile = min(512, own)

    def partial_sums(owner, store):
        @pl.loop(0, own // tile)
        def _(t):
            rows = block(owner * (own // tile) + t, tile)
            store(
                block(t, tile),
                jnp.dot(s.energy[rows, :], s.scaled[...], preferred_element_type=F32),
            )

    partner = pts + 1 - 2 * core
    x_copies = []
    order = [d % chips for d in range(1, chips + 1)]
    for d in order:

        def to_pair(rows, values, d=d):
            s.pair_send[d, rows, :] = values.astype(BF16)

        partial_sums(((chip + d) % chips) * 2 + 1 - core, to_pair)
        x_copies.append(
            send(
                s.pair_send.at[d],
                s.pair_recv.at[d],
                s.px_send.at[d],
                s.px_recv.at[d],
                "pts",
                partner,
            )
        )
    y_copies = []
    for n, d in enumerate(order):

        def to_mine(rows, values):
            s.mine[rows, :] = values

        owner = ((chip + d) % chips) * 2 + core
        partial_sums(owner, to_mine)
        x_copies[n].wait_recv()
        pair = s.mine[...] + s.pair_recv[d].astype(F32)
        if d:
            s.chip_send[d] = pair.astype(BF16)
            y_copies.append(
                send(
                    s.chip_send.at[d],
                    s.chip_recv.at[d],
                    s.py_send.at[d],
                    s.py_recv.at[d],
                    "pts",
                    owner,
                )
            )
        else:
            s.mine[...] = pair
    for copy in y_copies:
        copy.wait_recv()
    for j in range(own // LANES):
        rows = slice(j * LANES, (j + 1) * LANES)
        sums = s.mine[rows, :]
        for d in range(1, chips):
            sums += s.chip_recv[d, rows, :].astype(F32)
        wide = column_of(s.dense[pl.ds(pts * (own // LANES) + j, 1), :], LANES)
        out[rows, :] = rms_norm(sums * jnp.concatenate([wide] * (dp // LANES), axis=1))
    for copy in pending:
        copy.wait_send()
    settle()


def in_line(points, nlst):
    return nlst == 4 and points % (2 * LANES) == 0


def on_device(npts, nlst, tower_out, projection, centroids):
    points, feats = tower_out.shape
    lists, dp = centroids.shape
    share = points // nlst
    own = lists // npts
    chips = npts // 2
    chunks = 2 if share % (2 * LANES) == 0 else 1
    vmem = pl.BlockSpec(memory_space=pltpu.VMEM)
    hbm = pl.BlockSpec(memory_space=pl.ANY)
    sem = pltpu.SemaphoreType.DMA
    scratch = dict(
        tower=pltpu.VMEM((points, feats), BF16),
        proj=pltpu.VMEM((feats, dp), BF16),
        unit=pltpu.VMEM((lists, dp), BF16),
        energy=pltpu.VMEM((lists, points), BF16),
        lane_sums=pltpu.VMEM((lists, LANES), F32),
        dense=pltpu.VMEM((lists // LANES, LANES), F32),
        col_sums=pltpu.VMEM((ITERS, npts, lists // LANES, LANES), BF16),
        row_sums=pltpu.VMEM((ITERS, nlst, points // LANES, LANES), F32),
        scaled=pltpu.VMEM((points, dp), BF16),
        pair_send=pltpu.VMEM((chips, own, dp), BF16),
        pair_recv=pltpu.VMEM((chips, own, dp), BF16),
        chip_send=pltpu.VMEM((chips, own, dp), BF16),
        chip_recv=pltpu.VMEM((chips, own, dp), BF16),
        mine=pltpu.VMEM((own, dp), F32),
        load=sem((3,)),
        c_send=sem((ITERS, npts)),
        c_recv=sem((ITERS, npts)),
        r_send=sem((ITERS, nlst)),
        r_recv=sem((ITERS, nlst)),
        px_send=sem((chips,)),
        px_recv=sem((chips,)),
        py_send=sem((chips,)),
        py_recv=sem((chips,)),
    )
    if in_line(points, nlst):
        scratch.update(line_scratch(points, lists, feats, dp))
    else:
        scratch.update(any_scratch(points, lists, feats, dp, npts, nlst, chunks))
    centers, row_log = pl.pallas_call(
        functools.partial(kernel, npts, nlst, chunks, tuple(scratch)),
        out_shape=(
            jax.ShapeDtypeStruct((own, dp), F32),
            jax.ShapeDtypeStruct((points // LANES, LANES), F32),
        ),
        in_specs=[hbm] * 3,
        out_specs=(vmem, vmem),
        scratch_shapes=list(scratch.values()),
        compiler_params=pltpu.CompilerParams(
            collective_id=0, has_side_effects=True, vmem_limit_bytes=60000000
        ),
    )(tower_out, projection, centroids)
    return centers, row_log.reshape(points)


def solution(mesh):
    return jax.shard_map(
        functools.partial(on_device, mesh.shape["pts"], mesh.shape["lst"]),
        mesh=mesh,
        in_specs=(P("pts", "lst"), P("lst", None), P("lst", None)),
        out_specs=(P(("lst", "pts"), None), P("pts")),
        check_vma=False,
    )
```

```python
import functools
import math
from types import SimpleNamespace

import jax
import jax.numpy as jnp
from jax import lax
from jax.experimental import pallas as pl
from jax.experimental.pallas import tpu as pltpu
from jax.sharding import PartitionSpec as P

ITERS = 3
temper = 0.05
LANES = 128
AHEAD = 2
MESH = pl.DeviceIdType.MESH
F32 = jnp.float32
BF16 = jnp.bfloat16


def rms_norm(values):
    return values * lax.rsqrt(jnp.mean(values * values, axis=-1, keepdims=True) + 1e-06)


def column_of(row, rows):
    return jnp.broadcast_to(row, (rows, LANES)).T


def halved(values, rows):
    while values.shape[0] > rows:
        n = values.shape[0] // 2
        values = values[:n] + values[n:]
    return values


def added(terms):
    while len(terms) > 1:
        rest = terms[len(terms) // 2 * 2 :]
        terms = [terms[i] + terms[i + 1] for i in range(0, len(terms) - 1, 2)] + rest
    return terms[0]


def block(start, size):
    return pl.ds(pl.multiple_of(start * size, size), size)


def energy_block(s, gain, rows, cols, points):
    scores = lax.dot_general(
        s.unit[rows, :], points, (((1,), (1,)), ((), ())), preferred_element_type=F32
    )
    values = jnp.exp2(scores * gain)
    s.energy[rows, cols] = values.astype(BF16)
    width = values.shape[1] // LANES
    s.lane_sums[rows, :] += added([values[:, m * LANES : (m + 1) * LANES] for m in range(width)])


def unit_lists(s):
    lists = s.unit.shape[0]
    rows_each = min(256, lists)

    @pl.loop(0, lists // rows_each)
    def _(b):
        rows = block(b, rows_each)
        s.unit[rows, :] = rms_norm(s.unit[rows, :].astype(F32)).astype(BF16)
        s.lane_sums[rows, :] = jnp.zeros((rows_each, LANES), F32)


def line_gather(s, lst, gain, loads, arrive):
    points = s.tower.shape[0]
    lists = s.unit.shape[0]
    half = points // 2
    steps = half // LANES
    near = lst // 2
    far = 1 - near
    inner = (lst == 1) | (lst == 2)
    outer = jnp.logical_not(inner)
    inner_of_mine = 1 + near
    outer_of_mine = 3 * near
    other_inner = 2 - near

    def remote(src, dst, send_sem, recv_sem, target):
        return pltpu.make_async_remote_copy(
            src_ref=src,
            dst_ref=dst,
            send_sem=send_sem,
            recv_sem=recv_sem,
            device_id={"lst": target},
            device_id_type=MESH,
        )

    def feed(h, t):
        return remote(s.part.at[h, t], s.fed.at[h, t], s.f_send.at[h, t], s.f_recv.at[h, t], inner_of_mine)

    def cross(t):
        return remote(s.part.at[far, t], s.crossed.at[t], s.x_send.at[t], s.x_recv.at[t], other_inner)

    def back(u, h):
        return remote(
            s.normed.at[u, h], s.normed.at[u, h], s.b_send.at[u, h], s.n_recv.at[u, h], outer_of_mine
        )

    def across(u):
        return remote(
            s.normed.at[u, near], s.normed.at[u, near], s.a_send.at[u], s.n_recv.at[u, near], other_inner
        )

    def arrived(u, h):
        return remote(
            s.normed.at[u, h], s.normed.at[u, h], s.b_send.at[u, h], s.n_recv.at[u, h], other_inner
        )

    loads["proj"].wait()
    loads["tower"].wait()
    arrive()

    def partial(h, t):
        values = jnp.dot(
            s.tower[block(h * steps + t, LANES), :], s.proj[...], preferred_element_type=F32
        )

        @pl.when(outer)
        def _():
            s.part[h, t] = values.astype(BF16)
            feed(h, t).start()

        @pl.when(inner)
        def _():
            s.own[h, t] = values

    @pl.loop(0, steps + AHEAD)
    def _(t):
        @pl.when(t < steps)
        def _():
            partial(far, t)

        @pl.when(t >= AHEAD)
        def _():
            partial(near, t - AHEAD)

    e_rows = min(2048, lists)

    @pl.loop(0, steps + AHEAD + 1)
    def _(t):
        @pl.when(inner & (t < steps))
        def _():
            feed(far, t).wait_recv()
            s.part[far, t] = (s.own[far, t] + s.fed[far, t].astype(F32)).astype(BF16)
            cross(t).start()

        @pl.when(inner & (t >= AHEAD) & (t < steps + AHEAD))
        def _():
            u = t - AHEAD
            feed(near, u).wait_recv()
            cross(u).wait_recv()
            hidden = s.own[near, u] + s.fed[near, u].astype(F32) + s.crossed[u].astype(F32)
            s.normed[u, near] = rms_norm(hidden).astype(BF16)
            back(u, near).start()
            across(u).start()

        @pl.when(t == 1)
        def _():
            loads["cent"].wait()
            unit_lists(s)

        @pl.when(t > AHEAD)
        def _():
            u = t - AHEAD - 1

            @pl.when(inner)
            def _():
                arrived(u, far).wait_recv()
                back(u, far).start()

            @pl.when(outer)
            def _():
                arrived(u, near).wait_recv()
                arrived(u, far).wait_recv()

            @pl.loop(0, lists // e_rows)
            def _(b):
                rows = block(b, e_rows)
                pair = s.normed[u].reshape(2 * LANES, s.normed.shape[-1])
                energy_block(s, gain, rows, block(u, 2 * LANES), pair)

    def settle():
        @pl.loop(0, steps)
        def _(t):
            @pl.when(outer)
            def _():
                feed(far, t).wait_send()
                feed(near, t).wait_send()

            @pl.when(inner)
            def _():
                cross(t).wait_send()
                back(t, near).wait_send()
                back(t, far).wait_send()
                across(t).wait_send()

    def points_of(m):
        return s.normed[m // 2, m % 2]

    return settle, points_of, [h * steps + u for u in range(steps) for h in range(2)]


def line_scratch(points, lists, feats, dp):
    half = points // 2
    steps = half // LANES
    sem = pltpu.SemaphoreType.DMA
    return dict(
        own=pltpu.VMEM((2, steps, LANES, dp), F32),
        part=pltpu.VMEM((2, steps, LANES, dp), BF16),
        fed=pltpu.VMEM((2, steps, LANES, dp), BF16),
        crossed=pltpu.VMEM((steps, LANES, dp), BF16),
        normed=pltpu.VMEM((steps, 2, LANES, dp), BF16),
        f_send=sem((2, steps)),
        f_recv=sem((2, steps)),
        x_send=sem((steps,)),
        x_recv=sem((steps,)),
        b_send=sem((steps, 2)),
        a_send=sem((steps,)),
        n_recv=sem((steps, 2)),
    )


def any_gather(s, nlst, npts, lst, pts, send, chunks, gain, loads, arrive):
    points = s.tower.shape[0]
    lists = s.unit.shape[0]
    share = points // nlst
    feats = s.proj.shape[0]
    loads["proj"].wait()
    loads["tower"].wait()
    arrive()
    piece = feats // npts
    sliced = piece % 16 == 0
    piece_rows = block(pts, piece) if sliced else pl.ds(0, feats)
    p_copies = [
        send(
            s.proj.at[piece_rows],
            s.pfull.at[d, piece_rows],
            s.p_send.at[d],
            s.p_recv.at[d],
            "lst",
            (lst + d) % nlst,
        )
        for d in range(1, nlst)
    ]
    chunk = share // chunks
    t_copies = []
    for c in range(chunks):
        for d in range(1, nlst):
            z = (lst + d) % nlst
            t_copies.append(
                send(
                    s.tower.at[block(z * chunks + c, chunk)],
                    s.full.at[c, d],
                    s.t_send.at[c, d],
                    s.t_recv.at[c, d],
                    "lst",
                    z,
                )
            )
    loads["cent"].wait()
    unit_lists(s)

    for copy in p_copies:
        copy.wait_recv()
    if sliced:
        q_copies = [
            send(
                s.pfull.at[pl.ds(1, nlst - 1), piece_rows],
                s.pfull.at[pl.ds(1, nlst - 1), piece_rows],
                s.q_send.at[d],
                s.q_recv.at[d],
                "pts",
                (pts + d) % npts,
            )
            for d in range(1, npts)
        ]
        for copy in q_copies:
            copy.wait_recv()

    def hop(c, origin, left):
        side = 0 if left else 1
        return pltpu.make_async_remote_copy(
            src_ref=s.normed.at[c, origin],
            dst_ref=s.normed.at[c, origin],
            send_sem=s.n_send.at[side, c, origin],
            recv_sem=s.n_recv.at[c, origin],
            device_id={"lst": lst - 1 if left else lst + 1},
            device_id_type=MESH,
        )

    has_left = lst > 0
    has_right = lst < nlst - 1
    for c in range(chunks):
        hidden = jnp.dot(
            s.tower[block(lst * chunks + c, chunk), :], s.proj[...], preferred_element_type=F32
        )
        for d in range(1, nlst):
            t_copies[c * (nlst - 1) + d - 1].wait_recv()
            hidden += jnp.dot(s.full[c, d], s.pfull[d], preferred_element_type=F32)
        s.normed[c, lst] = rms_norm(hidden).astype(BF16)

        @pl.when(has_left)
        def _(c=c):
            hop(c, lst, True).start()

        @pl.when(has_right)
        def _(c=c):
            hop(c, lst, False).start()

    e_rows = min(1024, lists)
    step = min(256, chunk)
    per_share = share // step
    per_chunk = chunk // step

    def energy_of(c, origin):
        @pl.loop(0, lists // e_rows)
        def _(b):
            rows = block(b, e_rows)
            for k in range(per_chunk):
                cols = block(origin * per_share + c * per_chunk + k, step)
                energy_block(s, gain, rows, cols, s.normed[c, origin, k * step : (k + 1) * step, :])

    paired = jnp.minimum(lst, nlst - 1 - lst)
    for n in range(nlst):
        close = (n + 1) // 2
        away = n - paired
        in_pairs = lst - close if n % 2 else lst + close
        beyond = jnp.where(has_right & (lst < nlst - 1 - lst), lst + away, lst - away)
        origin = jnp.where(n <= 2 * paired, in_pairs, beyond) if n else lst
        for c in range(chunks):
            if n:
                hop(c, origin, True).wait_recv()

                @pl.when((origin < lst) & has_right)
                def _(c=c, origin=origin):
                    hop(c, origin, False).start()

                @pl.when((origin > lst) & has_left)
                def _(c=c, origin=origin):
                    hop(c, origin, True).start()

            energy_of(c, origin)

    def settle():
        for z in range(nlst):
            for c in range(chunks):

                @pl.when((z <= lst) & has_right)
                def _(c=c, z=z):
                    hop(c, z, False).wait_send()

                @pl.when((z >= lst) & has_left)
                def _(c=c, z=z):
                    hop(c, z, True).wait_send()

    def points_of(m):
        d, k = divmod(m * LANES, share)
        c, k = divmod(k, chunk)
        return s.normed[c, d, k : k + LANES, :]

    return settle, points_of, list(range(points // LANES))


def any_scratch(points, lists, feats, dp, npts, nlst, chunks):
    chunk = points // nlst // chunks
    sem = pltpu.SemaphoreType.DMA
    return dict(
        full=pltpu.VMEM((chunks, nlst, chunk, feats), BF16),
        pfull=pltpu.VMEM((nlst, feats, dp), BF16),
        normed=pltpu.VMEM((chunks, nlst, chunk, dp), BF16),
        t_send=sem((chunks, nlst)),
        t_recv=sem((chunks, nlst)),
        p_send=sem((nlst,)),
        p_recv=sem((nlst,)),
        q_send=sem((npts,)),
        q_recv=sem((npts,)),
        n_send=sem((2, chunks, nlst)),
        n_recv=sem((chunks, nlst)),
    )


def kernel(npts, nlst, chunks, names, tower, proj, cent, out, row_log, *scratch):
    s = SimpleNamespace(**dict(zip(names, scratch)))
    pts = lax.axis_index("pts")
    lst = lax.axis_index("lst")
    lists, dp = s.unit.shape
    points = s.tower.shape[0]
    own = lists // npts
    chips = npts // 2
    core = pts % 2
    chip = pts // 2
    balance = (points * npts) / (lists * nlst)
    list_blocks = lists // LANES
    point_blocks = points // LANES

    loads = {
        "proj": pltpu.make_async_copy(proj, s.proj, s.load.at[0]),
        "tower": pltpu.make_async_copy(tower, s.tower, s.load.at[1]),
        "cent": pltpu.make_async_copy(cent, s.unit, s.load.at[2]),
    }
    for copy in loads.values():
        copy.start()

    barrier = pltpu.get_barrier_semaphore()
    for d in range(1, nlst):
        pl.semaphore_signal(
            barrier, inc=1, device_id={"lst": (lst + d) % nlst}, device_id_type=MESH
        )
    for d in range(1, npts):
        pl.semaphore_signal(
            barrier, inc=1, device_id={"pts": (pts + d) % npts}, device_id_type=MESH
        )

    def arrive():
        pl.semaphore_wait(barrier, nlst + npts - 2)

    pending = []

    def remote(src, dst, send_sem, recv_sem, axis, target):
        return pltpu.make_async_remote_copy(
            src_ref=src,
            dst_ref=dst,
            send_sem=send_sem,
            recv_sem=recv_sem,
            device_id={axis: target},
            device_id_type=MESH,
        )

    def send(*what):
        copy = remote(*what)
        copy.start()
        pending.append(copy)
        return copy

    gain = 1.0 / (math.log(2.0) * dp * temper)
    if in_line(points, nlst):
        settle, points_of, place = line_gather(s, lst, gain, loads, arrive)
    else:
        settle, points_of, place = any_gather(
            s, nlst, npts, lst, pts, send, chunks, gain, loads, arrive
        )

    def lane_dense(sums):
        return jnp.sum(sums.T, axis=0, keepdims=True)

    @pl.loop(0, list_blocks, unroll=4)
    def _(b):
        s.dense[pl.ds(b, 1), :] = lane_dense(s.lane_sums[block(b, LANES), :])

    @pl.loop(0, ITERS)
    def _(sweep):
        s.col_sums[sweep, 0] = s.dense[...].astype(BF16)
        c_copies = [
            remote(
                s.col_sums.at[sweep, 0],
                s.col_sums.at[sweep, d],
                s.c_send.at[sweep, d],
                s.c_recv.at[sweep, d],
                "pts",
                (pts + d) % npts,
            )
            for d in range(1, npts)
        ]
        for copy in c_copies:
            copy.start()
        for copy in c_copies:
            copy.wait_recv()
        total = added([s.col_sums[sweep, d].astype(F32) for d in range(npts)])
        s.dense[...] = balance / total

        def row_step(b, acc):
            rows = block(b, LANES)
            wide = column_of(s.dense[pl.ds(b, 1), :], LANES).astype(BF16)
            parts = []
            for m in range(point_blocks):
                term = halved(s.energy[rows, m * LANES : (m + 1) * LANES] * wide, 16).astype(F32)
                parts.append(acc[m] + halved(term, 8))
            return tuple(parts)

        acc = lax.fori_loop(
            0,
            list_blocks,
            row_step,
            tuple(jnp.zeros((8, LANES), F32) for _ in range(point_blocks)),
            unroll=4,
        )
        s.row_sums[sweep, 0] = jnp.concatenate(
            [jnp.sum(part, axis=0, keepdims=True) for part in acc], axis=0
        )
        r_copies = [
            remote(
                s.row_sums.at[sweep, 0],
                s.row_sums.at[sweep, d],
                s.r_send.at[sweep, d],
                s.r_recv.at[sweep, d],
                "lst",
                (lst + d) % nlst,
            )
            for d in range(1, nlst)
        ]
        for copy in r_copies:
            copy.start()
        for copy in r_copies:
            copy.wait_recv()
        s.row_scale[...] = 1.0 / added([s.row_sums[sweep, d] for d in range(nlst)])

        @pl.when(sweep < ITERS - 1)
        def _():
            wide = [
                jnp.broadcast_to(s.row_scale[m : m + 1, :], (16, LANES)).astype(BF16)
                for m in range(point_blocks)
            ]

            @pl.loop(0, list_blocks, unroll=4)
            def _(b):
                groups = []
                for q in range(LANES // 16):
                    rows = block(b * (LANES // 16) + q, 16)
                    groups.append(
                        added(
                            [
                                s.energy[rows, m * LANES : (m + 1) * LANES] * wide[m]
                                for m in range(point_blocks)
                            ]
                        )
                    )
                s.dense[pl.ds(b, 1), :] = lane_dense(jnp.concatenate(groups, axis=0).astype(F32))

        for copy in c_copies + r_copies:
            copy.wait_send()

    row_scale = s.row_scale[...]
    logs = jnp.log(row_scale)
    for m in range(point_blocks):
        row_log[place[m] : place[m] + 1, :] = logs[m : m + 1, :]

    for m in range(point_blocks):
        wide = column_of(row_scale[m : m + 1, :], LANES)
        values = points_of(m).astype(F32)
        for h in range(dp // LANES):
            lanes = slice(h * LANES, (h + 1) * LANES)
            s.scaled[m * LANES : (m + 1) * LANES, lanes] = (values[:, lanes] * wide).astype(BF16)

    tile = min(512, own)

    def chip_at(d):
        if chips == 4:
            return (chip // 2 + d // 2) % 2 * 2 + (chip + d) % 2
        return (chip + d) % chips

    def to_pair(d):
        return remote(
            s.pair_send.at[d],
            s.pair_recv.at[d],
            s.px_send.at[d],
            s.px_recv.at[d],
            "pts",
            pts + 1 - 2 * core,
        )

    def to_chip(d):
        return remote(
            s.chip_send.at[d],
            s.chip_recv.at[d],
            s.py_send.at[d],
            s.py_recv.at[d],
            "pts",
            chip_at(d) * 2 + core,
        )

    last = 2 * chips - 1

    @pl.loop(0, 2 * chips)
    def _(k):
        for_pair = (k == 0) | ((k % 2 == 1) & (k < last))
        turn = jnp.where(for_pair, (k + 1) // 2, jnp.where(k == last, chips - 1, k // 2 - 1))
        d = chips - 1 - turn
        owner = chip_at(d) * 2 + jnp.where(for_pair, 1 - core, core)

        @pl.loop(0, own // tile)
        def _(t):
            s.mine[block(t, tile), :] = jnp.dot(
                s.energy[block(owner * (own // tile) + t, tile), :],
                s.scaled[...],
                preferred_element_type=F32,
            )

        @pl.when(for_pair)
        def _():
            s.pair_send[d] = s.mine[...].astype(BF16)
            to_pair(d).start()

        @pl.when(jnp.logical_not(for_pair))
        def _():
            to_pair(d).wait_recv()
            both = s.mine[...] + s.pair_recv[d].astype(F32)

            @pl.when(d > 0)
            def _():
                s.chip_send[d] = both.astype(BF16)
                to_chip(d).start()

            @pl.when(d == 0)
            def _():
                s.mine[...] = both

    for d in range(1, chips):
        to_chip(d).wait_recv()
    for j in range(own // LANES):
        rows = slice(j * LANES, (j + 1) * LANES)
        sums = s.mine[rows, :]
        for d in range(1, chips):
            sums += s.chip_recv[d, rows, :].astype(F32)
        wide = column_of(s.dense[pl.ds(pts * (own // LANES) + j, 1), :], LANES)
        out[rows, :] = rms_norm(sums * jnp.concatenate([wide] * (dp // LANES), axis=1))
    for copy in pending:
        copy.wait_send()
    for d in range(chips):
        to_pair(d).wait_send()
    for d in range(1, chips):
        to_chip(d).wait_send()
    settle()


def in_line(points, nlst):
    return nlst == 4 and points % (2 * LANES) == 0


def on_device(npts, nlst, tower_out, projection, centroids):
    points, feats = tower_out.shape
    lists, dp = centroids.shape
    share = points // nlst
    own = lists // npts
    chips = npts // 2
    chunks = 2 if share % (2 * LANES) == 0 else 1
    vmem = pl.BlockSpec(memory_space=pltpu.VMEM)
    hbm = pl.BlockSpec(memory_space=pl.ANY)
    sem = pltpu.SemaphoreType.DMA
    scratch = dict(
        tower=pltpu.VMEM((points, feats), BF16),
        proj=pltpu.VMEM((feats, dp), BF16),
        unit=pltpu.VMEM((lists, dp), BF16),
        energy=pltpu.VMEM((lists, points), BF16),
        lane_sums=pltpu.VMEM((lists, LANES), F32),
        row_scale=pltpu.VMEM((points // LANES, LANES), F32),
        dense=pltpu.VMEM((lists // LANES, LANES), F32),
        col_sums=pltpu.VMEM((ITERS, npts, lists // LANES, LANES), BF16),
        row_sums=pltpu.VMEM((ITERS, nlst, points // LANES, LANES), F32),
        scaled=pltpu.VMEM((points, dp), BF16),
        pair_send=pltpu.VMEM((chips, own, dp), BF16),
        pair_recv=pltpu.VMEM((chips, own, dp), BF16),
        chip_send=pltpu.VMEM((chips, own, dp), BF16),
        chip_recv=pltpu.VMEM((chips, own, dp), BF16),
        mine=pltpu.VMEM((own, dp), F32),
        load=sem((3,)),
        c_send=sem((ITERS, npts)),
        c_recv=sem((ITERS, npts)),
        r_send=sem((ITERS, nlst)),
        r_recv=sem((ITERS, nlst)),
        px_send=sem((chips,)),
        px_recv=sem((chips,)),
        py_send=sem((chips,)),
        py_recv=sem((chips,)),
    )
    if in_line(points, nlst):
        scratch.update(line_scratch(points, lists, feats, dp))
    else:
        scratch.update(any_scratch(points, lists, feats, dp, npts, nlst, chunks))
    centers, row_log = pl.pallas_call(
        functools.partial(kernel, npts, nlst, chunks, tuple(scratch)),
        out_shape=(
            jax.ShapeDtypeStruct((own, dp), F32),
            jax.ShapeDtypeStruct((points // LANES, LANES), F32),
        ),
        in_specs=[hbm] * 3,
        out_specs=(vmem, vmem),
        scratch_shapes=list(scratch.values()),
        compiler_params=pltpu.CompilerParams(
            collective_id=0, has_side_effects=True, vmem_limit_bytes=60000000
        ),
    )(tower_out, projection, centroids)
    return centers, row_log.reshape(points)


def solution(mesh):
    return jax.shard_map(
        functools.partial(on_device, mesh.shape["pts"], mesh.shape["lst"]),
        mesh=mesh,
        in_specs=(P("pts", "lst"), P("lst", None), P("lst", None)),
        out_specs=(P(("lst", "pts"), None), P("pts")),
        check_vma=False,
    )
```

```python
import functools
import math
from types import SimpleNamespace

import jax
import jax.numpy as jnp
from jax import lax
from jax.experimental import pallas as pl
from jax.experimental.pallas import tpu as pltpu
from jax.sharding import PartitionSpec as P

ITERS = 3
temper = 0.05
LANES = 128
AHEAD = 2
MESH = pl.DeviceIdType.MESH
F32 = jnp.float32
BF16 = jnp.bfloat16


def rms_norm(values):
    return values * lax.rsqrt(jnp.mean(values * values, axis=-1, keepdims=True) + 1e-06)


def column_of(row, rows):
    return jnp.broadcast_to(row, (rows, LANES)).T


def added(terms):
    while len(terms) > 1:
        rest = terms[len(terms) // 2 * 2 :]
        terms = [terms[i] + terms[i + 1] for i in range(0, len(terms) - 1, 2)] + rest
    return terms[0]


def block(start, size):
    return pl.ds(pl.multiple_of(start * size, size), size)


def energy_block(s, gain, rows, cols, points):
    scores = lax.dot_general(
        s.unit[rows, :], points, (((1,), (1,)), ((), ())), preferred_element_type=F32
    )
    values = jnp.exp2(scores * gain)
    s.energy[rows, cols] = values.astype(BF16)
    width = values.shape[1] // LANES
    s.lane_sums[rows, :] += added([values[:, m * LANES : (m + 1) * LANES] for m in range(width)])


def unit_lists(s):
    lists = s.unit.shape[0]
    rows_each = min(256, lists)

    @pl.loop(0, lists // rows_each)
    def _(b):
        rows = block(b, rows_each)
        s.unit[rows, :] = rms_norm(s.unit[rows, :].astype(F32)).astype(BF16)
        s.lane_sums[rows, :] = jnp.zeros((rows_each, LANES), F32)


def line_gather(s, lst, gain, loads, arrive):
    points = s.tower.shape[0]
    lists = s.unit.shape[0]
    half = points // 2
    steps = half // LANES
    near = lst // 2
    far = 1 - near
    inner = (lst == 1) | (lst == 2)
    outer = jnp.logical_not(inner)
    inner_of_mine = 1 + near
    outer_of_mine = 3 * near
    other_inner = 2 - near

    def remote(src, dst, send_sem, recv_sem, target):
        return pltpu.make_async_remote_copy(
            src_ref=src,
            dst_ref=dst,
            send_sem=send_sem,
            recv_sem=recv_sem,
            device_id={"lst": target},
            device_id_type=MESH,
        )

    def feed(h, t):
        return remote(s.part.at[h, t], s.fed.at[h, t], s.f_send.at[h, t], s.f_recv.at[h, t], inner_of_mine)

    def cross(t):
        return remote(s.part.at[far, t], s.crossed.at[t], s.x_send.at[t], s.x_recv.at[t], other_inner)

    def back(u, h):
        return remote(
            s.normed.at[u, h], s.normed.at[u, h], s.b_send.at[u, h], s.n_recv.at[u, h], outer_of_mine
        )

    def across(u):
        return remote(
            s.normed.at[u, near], s.normed.at[u, near], s.a_send.at[u], s.n_recv.at[u, near], other_inner
        )

    def arrived(u, h):
        return remote(
            s.normed.at[u, h], s.normed.at[u, h], s.b_send.at[u, h], s.n_recv.at[u, h], other_inner
        )

    loads["proj"].wait()
    loads["tower"].wait()
    arrive()

    def partial(h, t):
        values = jnp.dot(
            s.tower[block(h * steps + t, LANES), :], s.proj[...], preferred_element_type=F32
        )

        @pl.when(outer)
        def _():
            s.part[h, t] = values.astype(BF16)
            feed(h, t).start()

        @pl.when(inner)
        def _():
            s.own[h, t] = values

    @pl.loop(0, steps + AHEAD)
    def _(t):
        @pl.when(t < steps)
        def _():
            partial(far, t)

        @pl.when(t >= AHEAD)
        def _():
            partial(near, t - AHEAD)

    e_rows = min(2048, lists)

    @pl.loop(0, steps + AHEAD + 1)
    def _(t):
        @pl.when(inner & (t < steps))
        def _():
            feed(far, t).wait_recv()
            s.part[far, t] = (s.own[far, t] + s.fed[far, t].astype(F32)).astype(BF16)
            cross(t).start()

        @pl.when(inner & (t >= AHEAD) & (t < steps + AHEAD))
        def _():
            u = t - AHEAD
            feed(near, u).wait_recv()
            cross(u).wait_recv()
            hidden = s.own[near, u] + s.fed[near, u].astype(F32) + s.crossed[u].astype(F32)
            s.normed[u, near] = rms_norm(hidden).astype(BF16)
            back(u, near).start()
            across(u).start()

        @pl.when(t == 1)
        def _():
            loads["cent"].wait()
            unit_lists(s)

        @pl.when(t > AHEAD)
        def _():
            u = t - AHEAD - 1

            @pl.when(inner)
            def _():
                arrived(u, far).wait_recv()
                back(u, far).start()

            @pl.when(outer)
            def _():
                arrived(u, near).wait_recv()
                arrived(u, far).wait_recv()

            @pl.loop(0, lists // e_rows)
            def _(b):
                rows = block(b, e_rows)
                pair = s.normed[u].reshape(2 * LANES, s.normed.shape[-1])
                energy_block(s, gain, rows, block(u, 2 * LANES), pair)

    def settle():
        @pl.loop(0, steps)
        def _(t):
            @pl.when(outer)
            def _():
                feed(far, t).wait_send()
                feed(near, t).wait_send()

            @pl.when(inner)
            def _():
                cross(t).wait_send()
                back(t, near).wait_send()
                back(t, far).wait_send()
                across(t).wait_send()

    def points_of(m):
        return s.normed[m // 2, m % 2]

    return settle, points_of, [h * steps + u for u in range(steps) for h in range(2)]


def line_scratch(points, lists, feats, dp):
    half = points // 2
    steps = half // LANES
    sem = pltpu.SemaphoreType.DMA
    return dict(
        own=pltpu.VMEM((2, steps, LANES, dp), F32),
        part=pltpu.VMEM((2, steps, LANES, dp), BF16),
        fed=pltpu.VMEM((2, steps, LANES, dp), BF16),
        crossed=pltpu.VMEM((steps, LANES, dp), BF16),
        normed=pltpu.VMEM((steps, 2, LANES, dp), BF16),
        f_send=sem((2, steps)),
        f_recv=sem((2, steps)),
        x_send=sem((steps,)),
        x_recv=sem((steps,)),
        b_send=sem((steps, 2)),
        a_send=sem((steps,)),
        n_recv=sem((steps, 2)),
    )


def any_gather(s, nlst, npts, lst, pts, send, chunks, gain, loads, arrive):
    points = s.tower.shape[0]
    lists = s.unit.shape[0]
    share = points // nlst
    feats = s.proj.shape[0]
    loads["proj"].wait()
    loads["tower"].wait()
    arrive()
    piece = feats // npts
    sliced = piece % 16 == 0
    piece_rows = block(pts, piece) if sliced else pl.ds(0, feats)
    p_copies = [
        send(
            s.proj.at[piece_rows],
            s.pfull.at[d, piece_rows],
            s.p_send.at[d],
            s.p_recv.at[d],
            "lst",
            (lst + d) % nlst,
        )
        for d in range(1, nlst)
    ]
    chunk = share // chunks
    t_copies = []
    for c in range(chunks):
        for d in range(1, nlst):
            z = (lst + d) % nlst
            t_copies.append(
                send(
                    s.tower.at[block(z * chunks + c, chunk)],
                    s.full.at[c, d],
                    s.t_send.at[c, d],
                    s.t_recv.at[c, d],
                    "lst",
                    z,
                )
            )
    loads["cent"].wait()
    unit_lists(s)

    for copy in p_copies:
        copy.wait_recv()
    if sliced:
        q_copies = [
            send(
                s.pfull.at[pl.ds(1, nlst - 1), piece_rows],
                s.pfull.at[pl.ds(1, nlst - 1), piece_rows],
                s.q_send.at[d],
                s.q_recv.at[d],
                "pts",
                (pts + d) % npts,
            )
            for d in range(1, npts)
        ]
        for copy in q_copies:
            copy.wait_recv()

    def hop(c, origin, left):
        side = 0 if left else 1
        return pltpu.make_async_remote_copy(
            src_ref=s.normed.at[c, origin],
            dst_ref=s.normed.at[c, origin],
            send_sem=s.n_send.at[side, c, origin],
            recv_sem=s.n_recv.at[c, origin],
            device_id={"lst": lst - 1 if left else lst + 1},
            device_id_type=MESH,
        )

    has_left = lst > 0
    has_right = lst < nlst - 1
    for c in range(chunks):
        hidden = jnp.dot(
            s.tower[block(lst * chunks + c, chunk), :], s.proj[...], preferred_element_type=F32
        )
        for d in range(1, nlst):
            t_copies[c * (nlst - 1) + d - 1].wait_recv()
            hidden += jnp.dot(s.full[c, d], s.pfull[d], preferred_element_type=F32)
        s.normed[c, lst] = rms_norm(hidden).astype(BF16)

        @pl.when(has_left)
        def _(c=c):
            hop(c, lst, True).start()

        @pl.when(has_right)
        def _(c=c):
            hop(c, lst, False).start()

    e_rows = min(1024, lists)
    step = min(256, chunk)
    per_share = share // step
    per_chunk = chunk // step

    def energy_of(c, origin):
        @pl.loop(0, lists // e_rows)
        def _(b):
            rows = block(b, e_rows)
            for k in range(per_chunk):
                cols = block(origin * per_share + c * per_chunk + k, step)
                energy_block(s, gain, rows, cols, s.normed[c, origin, k * step : (k + 1) * step, :])

    paired = jnp.minimum(lst, nlst - 1 - lst)
    for n in range(nlst):
        close = (n + 1) // 2
        away = n - paired
        in_pairs = lst - close if n % 2 else lst + close
        beyond = jnp.where(has_right & (lst < nlst - 1 - lst), lst + away, lst - away)
        origin = jnp.where(n <= 2 * paired, in_pairs, beyond) if n else lst
        for c in range(chunks):
            if n:
                hop(c, origin, True).wait_recv()

                @pl.when((origin < lst) & has_right)
                def _(c=c, origin=origin):
                    hop(c, origin, False).start()

                @pl.when((origin > lst) & has_left)
                def _(c=c, origin=origin):
                    hop(c, origin, True).start()

            energy_of(c, origin)

    def settle():
        for z in range(nlst):
            for c in range(chunks):

                @pl.when((z <= lst) & has_right)
                def _(c=c, z=z):
                    hop(c, z, False).wait_send()

                @pl.when((z >= lst) & has_left)
                def _(c=c, z=z):
                    hop(c, z, True).wait_send()

    def points_of(m):
        d, k = divmod(m * LANES, share)
        c, k = divmod(k, chunk)
        return s.normed[c, d, k : k + LANES, :]

    return settle, points_of, list(range(points // LANES))


def any_scratch(points, lists, feats, dp, npts, nlst, chunks):
    chunk = points // nlst // chunks
    sem = pltpu.SemaphoreType.DMA
    return dict(
        full=pltpu.VMEM((chunks, nlst, chunk, feats), BF16),
        pfull=pltpu.VMEM((nlst, feats, dp), BF16),
        normed=pltpu.VMEM((chunks, nlst, chunk, dp), BF16),
        t_send=sem((chunks, nlst)),
        t_recv=sem((chunks, nlst)),
        p_send=sem((nlst,)),
        p_recv=sem((nlst,)),
        q_send=sem((npts,)),
        q_recv=sem((npts,)),
        n_send=sem((2, chunks, nlst)),
        n_recv=sem((chunks, nlst)),
    )


def kernel(npts, nlst, chunks, names, tower, proj, cent, out, row_log, *scratch):
    s = SimpleNamespace(**dict(zip(names, scratch)))
    pts = lax.axis_index("pts")
    lst = lax.axis_index("lst")
    lists, dp = s.unit.shape
    points = s.tower.shape[0]
    own = lists // npts
    chips = npts // 2
    core = pts % 2
    chip = pts // 2
    balance = (points * npts) / (lists * nlst)
    list_blocks = lists // LANES
    point_blocks = points // LANES

    loads = {
        "proj": pltpu.make_async_copy(proj, s.proj, s.load.at[0]),
        "tower": pltpu.make_async_copy(tower, s.tower, s.load.at[1]),
        "cent": pltpu.make_async_copy(cent, s.unit, s.load.at[2]),
    }
    for copy in loads.values():
        copy.start()

    barrier = pltpu.get_barrier_semaphore()
    for d in range(1, nlst):
        pl.semaphore_signal(
            barrier, inc=1, device_id={"lst": (lst + d) % nlst}, device_id_type=MESH
        )
    for d in range(1, npts):
        pl.semaphore_signal(
            barrier, inc=1, device_id={"pts": (pts + d) % npts}, device_id_type=MESH
        )

    def arrive():
        pl.semaphore_wait(barrier, nlst + npts - 2)

    pending = []

    def remote(src, dst, send_sem, recv_sem, axis, target):
        return pltpu.make_async_remote_copy(
            src_ref=src,
            dst_ref=dst,
            send_sem=send_sem,
            recv_sem=recv_sem,
            device_id={axis: target},
            device_id_type=MESH,
        )

    def send(*what):
        copy = remote(*what)
        copy.start()
        pending.append(copy)
        return copy

    gain = 1.0 / (math.log(2.0) * dp * temper)
    if in_line(points, nlst):
        settle, points_of, place = line_gather(s, lst, gain, loads, arrive)
    else:
        settle, points_of, place = any_gather(
            s, nlst, npts, lst, pts, send, chunks, gain, loads, arrive
        )

    def lane_dense(sums):
        return jnp.sum(sums.T, axis=0, keepdims=True)

    @pl.loop(0, list_blocks, unroll=4)
    def _(b):
        s.dense[pl.ds(b, 1), :] = lane_dense(s.lane_sums[block(b, LANES), :])

    @pl.loop(0, ITERS)
    def _(sweep):
        s.col_sums[sweep, 0] = s.dense[...].astype(BF16)
        c_copies = [
            remote(
                s.col_sums.at[sweep, 0],
                s.col_sums.at[sweep, d],
                s.c_send.at[sweep, d],
                s.c_recv.at[sweep, d],
                "pts",
                (pts + d) % npts,
            )
            for d in range(1, npts)
        ]
        for copy in c_copies:
            copy.start()
        for copy in c_copies:
            copy.wait_recv()
        total = added([s.col_sums[sweep, d].astype(F32) for d in range(npts)])
        s.dense[...] = balance / total

        depth = min(512, lists)
        acc = jnp.zeros((16, points), F32)
        for b in range(lists // depth):
            scales = [
                jnp.broadcast_to(s.dense[k : k + 1, :], (16, LANES)).astype(BF16)
                for k in range(b * (depth // LANES), (b + 1) * (depth // LANES))
            ]
            acc += jnp.dot(
                jnp.concatenate(scales, axis=1),
                s.energy[b * depth : (b + 1) * depth, :],
                preferred_element_type=F32,
            )
        s.row_sums[sweep, 0] = jnp.concatenate(
            [acc[0:1, m * LANES : (m + 1) * LANES] for m in range(point_blocks)], axis=0
        )
        r_copies = [
            remote(
                s.row_sums.at[sweep, 0],
                s.row_sums.at[sweep, d],
                s.r_send.at[sweep, d],
                s.r_recv.at[sweep, d],
                "lst",
                (lst + d) % nlst,
            )
            for d in range(1, nlst)
        ]
        for copy in r_copies:
            copy.start()
        for copy in r_copies:
            copy.wait_recv()
        s.row_scale[...] = 1.0 / added([s.row_sums[sweep, d] for d in range(nlst)])

        @pl.when(sweep < ITERS - 1)
        def _():
            wide = [
                jnp.broadcast_to(s.row_scale[m : m + 1, :], (16, LANES)).astype(BF16)
                for m in range(point_blocks)
            ]

            @pl.loop(0, list_blocks, unroll=4)
            def _(b):
                groups = []
                for q in range(LANES // 16):
                    rows = block(b * (LANES // 16) + q, 16)
                    groups.append(
                        added(
                            [
                                s.energy[rows, m * LANES : (m + 1) * LANES] * wide[m]
                                for m in range(point_blocks)
                            ]
                        )
                    )
                s.dense[pl.ds(b, 1), :] = lane_dense(jnp.concatenate(groups, axis=0).astype(F32))

        for copy in c_copies + r_copies:
            copy.wait_send()

    row_scale = s.row_scale[...]
    logs = jnp.log(row_scale)
    for m in range(point_blocks):
        row_log[place[m] : place[m] + 1, :] = logs[m : m + 1, :]

    for m in range(point_blocks):
        wide = column_of(row_scale[m : m + 1, :], LANES)
        values = points_of(m).astype(F32)
        for h in range(dp // LANES):
            lanes = slice(h * LANES, (h + 1) * LANES)
            s.scaled[m * LANES : (m + 1) * LANES, lanes] = (values[:, lanes] * wide).astype(BF16)

    tile = min(512, own)

    def chip_at(d):
        if chips == 4:
            return (chip // 2 + d // 2) % 2 * 2 + (chip + d) % 2
        return (chip + d) % chips

    def to_pair(d):
        return remote(
            s.pair_send.at[d],
            s.pair_recv.at[d],
            s.px_send.at[d],
            s.px_recv.at[d],
            "pts",
            pts + 1 - 2 * core,
        )

    def to_chip(d):
        return remote(
            s.chip_send.at[d],
            s.chip_recv.at[d],
            s.py_send.at[d],
            s.py_recv.at[d],
            "pts",
            chip_at(d) * 2 + core,
        )

    last = 2 * chips - 1

    @pl.loop(0, 2 * chips)
    def _(k):
        for_pair = (k == 0) | ((k % 2 == 1) & (k < last))
        turn = jnp.where(for_pair, (k + 1) // 2, jnp.where(k == last, chips - 1, k // 2 - 1))
        d = chips - 1 - turn
        owner = chip_at(d) * 2 + jnp.where(for_pair, 1 - core, core)

        @pl.loop(0, own // tile)
        def _(t):
            s.mine[block(t, tile), :] = jnp.dot(
                s.energy[block(owner * (own // tile) + t, tile), :],
                s.scaled[...],
                preferred_element_type=F32,
            )

        @pl.when(for_pair)
        def _():
            s.pair_send[d] = s.mine[...].astype(BF16)
            to_pair(d).start()

        @pl.when(jnp.logical_not(for_pair))
        def _():
            to_pair(d).wait_recv()
            both = s.mine[...] + s.pair_recv[d].astype(F32)

            @pl.when(d > 0)
            def _():
                s.chip_send[d] = both.astype(BF16)
                to_chip(d).start()

            @pl.when(d == 0)
            def _():
                s.mine[...] = both

    for d in range(1, chips):
        to_chip(d).wait_recv()
    for j in range(own // LANES):
        rows = slice(j * LANES, (j + 1) * LANES)
        sums = s.mine[rows, :]
        for d in range(1, chips):
            sums += s.chip_recv[d, rows, :].astype(F32)
        wide = column_of(s.dense[pl.ds(pts * (own // LANES) + j, 1), :], LANES)
        out[rows, :] = rms_norm(sums * jnp.concatenate([wide] * (dp // LANES), axis=1))
    for copy in pending:
        copy.wait_send()
    for d in range(chips):
        to_pair(d).wait_send()
    for d in range(1, chips):
        to_chip(d).wait_send()
    settle()


def in_line(points, nlst):
    return nlst == 4 and points % (2 * LANES) == 0


def on_device(npts, nlst, tower_out, projection, centroids):
    points, feats = tower_out.shape
    lists, dp = centroids.shape
    share = points // nlst
    own = lists // npts
    chips = npts // 2
    chunks = 2 if share % (2 * LANES) == 0 else 1
    vmem = pl.BlockSpec(memory_space=pltpu.VMEM)
    hbm = pl.BlockSpec(memory_space=pl.ANY)
    sem = pltpu.SemaphoreType.DMA
    scratch = dict(
        tower=pltpu.VMEM((points, feats), BF16),
        proj=pltpu.VMEM((feats, dp), BF16),
        unit=pltpu.VMEM((lists, dp), BF16),
        energy=pltpu.VMEM((lists, points), BF16),
        lane_sums=pltpu.VMEM((lists, LANES), F32),
        row_scale=pltpu.VMEM((points // LANES, LANES), F32),
        dense=pltpu.VMEM((lists // LANES, LANES), F32),
        col_sums=pltpu.VMEM((ITERS, npts, lists // LANES, LANES), BF16),
        row_sums=pltpu.VMEM((ITERS, nlst, points // LANES, LANES), F32),
        scaled=pltpu.VMEM((points, dp), BF16),
        pair_send=pltpu.VMEM((chips, own, dp), BF16),
        pair_recv=pltpu.VMEM((chips, own, dp), BF16),
        chip_send=pltpu.VMEM((chips, own, dp), BF16),
        chip_recv=pltpu.VMEM((chips, own, dp), BF16),
        mine=pltpu.VMEM((own, dp), F32),
        load=sem((3,)),
        c_send=sem((ITERS, npts)),
        c_recv=sem((ITERS, npts)),
        r_send=sem((ITERS, nlst)),
        r_recv=sem((ITERS, nlst)),
        px_send=sem((chips,)),
        px_recv=sem((chips,)),
        py_send=sem((chips,)),
        py_recv=sem((chips,)),
    )
    if in_line(points, nlst):
        scratch.update(line_scratch(points, lists, feats, dp))
    else:
        scratch.update(any_scratch(points, lists, feats, dp, npts, nlst, chunks))
    centers, row_log = pl.pallas_call(
        functools.partial(kernel, npts, nlst, chunks, tuple(scratch)),
        out_shape=(
            jax.ShapeDtypeStruct((own, dp), F32),
            jax.ShapeDtypeStruct((points // LANES, LANES), F32),
        ),
        in_specs=[hbm] * 3,
        out_specs=(vmem, vmem),
        scratch_shapes=list(scratch.values()),
        compiler_params=pltpu.CompilerParams(
            collective_id=0, has_side_effects=True, vmem_limit_bytes=60000000
        ),
    )(tower_out, projection, centroids)
    return centers, row_log.reshape(points)


def solution(mesh):
    return jax.shard_map(
        functools.partial(on_device, mesh.shape["pts"], mesh.shape["lst"]),
        mesh=mesh,
        in_specs=(P("pts", "lst"), P("lst", None), P("lst", None)),
        out_specs=(P(("lst", "pts"), None), P("pts")),
        check_vma=False,
    )
```

```python
import functools
import math
from types import SimpleNamespace

import jax
import jax.numpy as jnp
from jax import lax
from jax.experimental import pallas as pl
from jax.experimental.pallas import tpu as pltpu
from jax.sharding import PartitionSpec as P

ITERS = 3
temper = 0.05
LANES = 128
AHEAD = 2
MESH = pl.DeviceIdType.MESH
F32 = jnp.float32
BF16 = jnp.bfloat16


def rms_norm(values):
    return values * lax.rsqrt(jnp.mean(values * values, axis=-1, keepdims=True) + 1e-06)


def column_of(row, rows):
    return jnp.broadcast_to(row, (rows, LANES)).T


def added(terms):
    while len(terms) > 1:
        rest = terms[len(terms) // 2 * 2 :]
        terms = [terms[i] + terms[i + 1] for i in range(0, len(terms) - 1, 2)] + rest
    return terms[0]


def block(start, size):
    return pl.ds(pl.multiple_of(start * size, size), size)


def energy_block(s, gain, rows, cols, points):
    scores = lax.dot_general(
        s.unit[rows, :], points, (((1,), (1,)), ((), ())), preferred_element_type=F32
    )
    values = jnp.exp2(scores * gain)
    s.energy[rows, cols] = values.astype(BF16)
    width = values.shape[1] // LANES
    s.lane_sums[rows, :] += added([values[:, m * LANES : (m + 1) * LANES] for m in range(width)])


def unit_lists(s):
    lists = s.unit.shape[0]
    rows_each = min(256, lists)

    @pl.loop(0, lists // rows_each)
    def _(b):
        rows = block(b, rows_each)
        s.unit[rows, :] = rms_norm(s.unit[rows, :].astype(F32)).astype(BF16)
        s.lane_sums[rows, :] = jnp.zeros((rows_each, LANES), F32)


def line_gather(s, lst, gain, loads, arrive):
    points = s.tower.shape[0]
    lists = s.unit.shape[0]
    half = points // 2
    steps = half // LANES
    near = lst // 2
    far = 1 - near
    inner = (lst == 1) | (lst == 2)
    outer = jnp.logical_not(inner)
    inner_of_mine = 1 + near
    outer_of_mine = 3 * near
    other_inner = 2 - near

    def remote(src, dst, send_sem, recv_sem, target):
        return pltpu.make_async_remote_copy(
            src_ref=src,
            dst_ref=dst,
            send_sem=send_sem,
            recv_sem=recv_sem,
            device_id={"lst": target},
            device_id_type=MESH,
        )

    def feed(h, t):
        return remote(s.part.at[h, t], s.fed.at[h, t], s.f_send.at[h, t], s.f_recv.at[h, t], inner_of_mine)

    def cross(t):
        return remote(s.part.at[far, t], s.crossed.at[t], s.x_send.at[t], s.x_recv.at[t], other_inner)

    def back(u, h):
        return remote(
            s.normed.at[u, h], s.normed.at[u, h], s.b_send.at[u, h], s.n_recv.at[u, h], outer_of_mine
        )

    def across(u):
        return remote(
            s.normed.at[u, near], s.normed.at[u, near], s.a_send.at[u], s.n_recv.at[u, near], other_inner
        )

    def arrived(u, h):
        return remote(
            s.normed.at[u, h], s.normed.at[u, h], s.b_send.at[u, h], s.n_recv.at[u, h], other_inner
        )

    loads["proj"].wait()
    loads["tower"].wait()
    arrive()

    def partial(h, t):
        values = jnp.dot(
            s.tower[block(h * steps + t, LANES), :], s.proj[...], preferred_element_type=F32
        )

        @pl.when(outer)
        def _():
            s.part[h, t] = values.astype(BF16)
            feed(h, t).start()

        @pl.when(inner)
        def _():
            s.own[h, t] = values

    @pl.loop(0, steps + AHEAD)
    def _(t):
        @pl.when(t < steps)
        def _():
            partial(far, t)

        @pl.when(t >= AHEAD)
        def _():
            partial(near, t - AHEAD)

    e_rows = min(2048, lists)

    @pl.loop(0, steps + AHEAD + 1)
    def _(t):
        @pl.when(inner & (t < steps))
        def _():
            feed(far, t).wait_recv()
            s.part[far, t] = (s.own[far, t] + s.fed[far, t].astype(F32)).astype(BF16)
            cross(t).start()

        @pl.when(inner & (t >= AHEAD) & (t < steps + AHEAD))
        def _():
            u = t - AHEAD
            feed(near, u).wait_recv()
            cross(u).wait_recv()
            hidden = s.own[near, u] + s.fed[near, u].astype(F32) + s.crossed[u].astype(F32)
            s.normed[u, near] = rms_norm(hidden).astype(BF16)
            back(u, near).start()
            across(u).start()

        @pl.when(t == 1)
        def _():
            loads["cent"].wait()
            unit_lists(s)

        @pl.when(t > AHEAD)
        def _():
            u = t - AHEAD - 1

            @pl.when(inner)
            def _():
                arrived(u, far).wait_recv()
                back(u, far).start()

            @pl.when(outer)
            def _():
                arrived(u, near).wait_recv()
                arrived(u, far).wait_recv()

            @pl.loop(0, lists // e_rows)
            def _(b):
                rows = block(b, e_rows)
                pair = s.normed[u].reshape(2 * LANES, s.normed.shape[-1])
                energy_block(s, gain, rows, block(u, 2 * LANES), pair)

    def settle():
        @pl.loop(0, steps)
        def _(t):
            @pl.when(outer)
            def _():
                feed(far, t).wait_send()
                feed(near, t).wait_send()

            @pl.when(inner)
            def _():
                cross(t).wait_send()
                back(t, near).wait_send()
                back(t, far).wait_send()
                across(t).wait_send()

    def points_of(m):
        return s.normed[m // 2, m % 2]

    return settle, points_of, [h * steps + u for u in range(steps) for h in range(2)]


def line_scratch(points, lists, feats, dp):
    half = points // 2
    steps = half // LANES
    sem = pltpu.SemaphoreType.DMA
    return dict(
        own=pltpu.VMEM((2, steps, LANES, dp), F32),
        part=pltpu.VMEM((2, steps, LANES, dp), BF16),
        fed=pltpu.VMEM((2, steps, LANES, dp), BF16),
        crossed=pltpu.VMEM((steps, LANES, dp), BF16),
        normed=pltpu.VMEM((steps, 2, LANES, dp), BF16),
        f_send=sem((2, steps)),
        f_recv=sem((2, steps)),
        x_send=sem((steps,)),
        x_recv=sem((steps,)),
        b_send=sem((steps, 2)),
        a_send=sem((steps,)),
        n_recv=sem((steps, 2)),
    )


def any_gather(s, nlst, npts, lst, pts, send, chunks, gain, loads, arrive):
    points = s.tower.shape[0]
    lists = s.unit.shape[0]
    share = points // nlst
    feats = s.proj.shape[0]
    loads["proj"].wait()
    loads["tower"].wait()
    arrive()
    piece = feats // npts
    sliced = piece % 16 == 0
    piece_rows = block(pts, piece) if sliced else pl.ds(0, feats)
    p_copies = [
        send(
            s.proj.at[piece_rows],
            s.pfull.at[d, piece_rows],
            s.p_send.at[d],
            s.p_recv.at[d],
            "lst",
            (lst + d) % nlst,
        )
        for d in range(1, nlst)
    ]
    chunk = share // chunks
    t_copies = []
    for c in range(chunks):
        for d in range(1, nlst):
            z = (lst + d) % nlst
            t_copies.append(
                send(
                    s.tower.at[block(z * chunks + c, chunk)],
                    s.full.at[c, d],
                    s.t_send.at[c, d],
                    s.t_recv.at[c, d],
                    "lst",
                    z,
                )
            )
    loads["cent"].wait()
    unit_lists(s)

    for copy in p_copies:
        copy.wait_recv()
    if sliced:
        q_copies = [
            send(
                s.pfull.at[pl.ds(1, nlst - 1), piece_rows],
                s.pfull.at[pl.ds(1, nlst - 1), piece_rows],
                s.q_send.at[d],
                s.q_recv.at[d],
                "pts",
                (pts + d) % npts,
            )
            for d in range(1, npts)
        ]
        for copy in q_copies:
            copy.wait_recv()

    def hop(c, origin, left):
        side = 0 if left else 1
        return pltpu.make_async_remote_copy(
            src_ref=s.normed.at[c, origin],
            dst_ref=s.normed.at[c, origin],
            send_sem=s.n_send.at[side, c, origin],
            recv_sem=s.n_recv.at[c, origin],
            device_id={"lst": lst - 1 if left else lst + 1},
            device_id_type=MESH,
        )

    has_left = lst > 0
    has_right = lst < nlst - 1
    for c in range(chunks):
        hidden = jnp.dot(
            s.tower[block(lst * chunks + c, chunk), :], s.proj[...], preferred_element_type=F32
        )
        for d in range(1, nlst):
            t_copies[c * (nlst - 1) + d - 1].wait_recv()
            hidden += jnp.dot(s.full[c, d], s.pfull[d], preferred_element_type=F32)
        s.normed[c, lst] = rms_norm(hidden).astype(BF16)

        @pl.when(has_left)
        def _(c=c):
            hop(c, lst, True).start()

        @pl.when(has_right)
        def _(c=c):
            hop(c, lst, False).start()

    e_rows = min(1024, lists)
    step = min(256, chunk)
    per_share = share // step
    per_chunk = chunk // step

    def energy_of(c, origin):
        @pl.loop(0, lists // e_rows)
        def _(b):
            rows = block(b, e_rows)
            for k in range(per_chunk):
                cols = block(origin * per_share + c * per_chunk + k, step)
                energy_block(s, gain, rows, cols, s.normed[c, origin, k * step : (k + 1) * step, :])

    paired = jnp.minimum(lst, nlst - 1 - lst)
    for n in range(nlst):
        close = (n + 1) // 2
        away = n - paired
        in_pairs = lst - close if n % 2 else lst + close
        beyond = jnp.where(has_right & (lst < nlst - 1 - lst), lst + away, lst - away)
        origin = jnp.where(n <= 2 * paired, in_pairs, beyond) if n else lst
        for c in range(chunks):
            if n:
                hop(c, origin, True).wait_recv()

                @pl.when((origin < lst) & has_right)
                def _(c=c, origin=origin):
                    hop(c, origin, False).start()

                @pl.when((origin > lst) & has_left)
                def _(c=c, origin=origin):
                    hop(c, origin, True).start()

            energy_of(c, origin)

    def settle():
        for z in range(nlst):
            for c in range(chunks):

                @pl.when((z <= lst) & has_right)
                def _(c=c, z=z):
                    hop(c, z, False).wait_send()

                @pl.when((z >= lst) & has_left)
                def _(c=c, z=z):
                    hop(c, z, True).wait_send()

    def points_of(m):
        d, k = divmod(m * LANES, share)
        c, k = divmod(k, chunk)
        return s.normed[c, d, k : k + LANES, :]

    return settle, points_of, list(range(points // LANES))


def any_scratch(points, lists, feats, dp, npts, nlst, chunks):
    chunk = points // nlst // chunks
    sem = pltpu.SemaphoreType.DMA
    return dict(
        full=pltpu.VMEM((chunks, nlst, chunk, feats), BF16),
        pfull=pltpu.VMEM((nlst, feats, dp), BF16),
        normed=pltpu.VMEM((chunks, nlst, chunk, dp), BF16),
        t_send=sem((chunks, nlst)),
        t_recv=sem((chunks, nlst)),
        p_send=sem((nlst,)),
        p_recv=sem((nlst,)),
        q_send=sem((npts,)),
        q_recv=sem((npts,)),
        n_send=sem((2, chunks, nlst)),
        n_recv=sem((chunks, nlst)),
    )


def kernel(npts, nlst, chunks, names, tower, proj, cent, out, row_log, *scratch):
    s = SimpleNamespace(**dict(zip(names, scratch)))
    pts = lax.axis_index("pts")
    lst = lax.axis_index("lst")
    lists, dp = s.unit.shape
    points = s.tower.shape[0]
    own = lists // npts
    chips = npts // 2
    core = pts % 2
    chip = pts // 2
    balance = (points * npts) / (lists * nlst)
    list_blocks = lists // LANES
    point_blocks = points // LANES

    loads = {
        "proj": pltpu.make_async_copy(proj, s.proj, s.load.at[0]),
        "tower": pltpu.make_async_copy(tower, s.tower, s.load.at[1]),
        "cent": pltpu.make_async_copy(cent, s.unit, s.load.at[2]),
    }
    for copy in loads.values():
        copy.start()

    barrier = pltpu.get_barrier_semaphore()
    for d in range(1, nlst):
        pl.semaphore_signal(
            barrier, inc=1, device_id={"lst": (lst + d) % nlst}, device_id_type=MESH
        )
    for d in range(1, npts):
        pl.semaphore_signal(
            barrier, inc=1, device_id={"pts": (pts + d) % npts}, device_id_type=MESH
        )

    def arrive():
        pl.semaphore_wait(barrier, nlst + npts - 2)

    pending = []

    def remote(src, dst, send_sem, recv_sem, axis, target):
        return pltpu.make_async_remote_copy(
            src_ref=src,
            dst_ref=dst,
            send_sem=send_sem,
            recv_sem=recv_sem,
            device_id={axis: target},
            device_id_type=MESH,
        )

    def send(*what):
        copy = remote(*what)
        copy.start()
        pending.append(copy)
        return copy

    gain = 1.0 / (math.log(2.0) * dp * temper)
    if in_line(points, nlst):
        settle, points_of, place = line_gather(s, lst, gain, loads, arrive)
    else:
        settle, points_of, place = any_gather(
            s, nlst, npts, lst, pts, send, chunks, gain, loads, arrive
        )

    ones = jnp.ones((LANES, LANES), BF16)
    diagonal = lax.broadcasted_iota(jnp.int32, (LANES, LANES), 0) == lax.broadcasted_iota(
        jnp.int32, (LANES, LANES), 1
    )

    def lane_dense(sums):
        wide = jnp.dot(sums, ones, preferred_element_type=F32)
        return jnp.sum(jnp.where(diagonal, wide, 0.0), axis=0, keepdims=True)

    @pl.loop(0, list_blocks, unroll=4)
    def _(b):
        s.dense[pl.ds(b, 1), :] = lane_dense(s.lane_sums[block(b, LANES), :].astype(BF16))

    @pl.loop(0, ITERS)
    def _(sweep):
        s.col_sums[sweep, 0] = s.dense[...].astype(BF16)
        c_copies = [
            remote(
                s.col_sums.at[sweep, 0],
                s.col_sums.at[sweep, d],
                s.c_send.at[sweep, d],
                s.c_recv.at[sweep, d],
                "pts",
                (pts + d) % npts,
            )
            for d in range(1, npts)
        ]
        for copy in c_copies:
            copy.start()
        for copy in c_copies:
            copy.wait_recv()
        total = added([s.col_sums[sweep, d].astype(F32) for d in range(npts)])
        s.dense[...] = balance / total

        depth = min(512, lists)
        acc = jnp.zeros((16, points), F32)
        for b in range(lists // depth):
            scales = [
                jnp.broadcast_to(s.dense[k : k + 1, :], (16, LANES)).astype(BF16)
                for k in range(b * (depth // LANES), (b + 1) * (depth // LANES))
            ]
            acc += jnp.dot(
                jnp.concatenate(scales, axis=1),
                s.energy[b * depth : (b + 1) * depth, :],
                preferred_element_type=F32,
            )
        s.row_sums[sweep, 0] = jnp.concatenate(
            [acc[0:1, m * LANES : (m + 1) * LANES] for m in range(point_blocks)], axis=0
        )
        r_copies = [
            remote(
                s.row_sums.at[sweep, 0],
                s.row_sums.at[sweep, d],
                s.r_send.at[sweep, d],
                s.r_recv.at[sweep, d],
                "lst",
                (lst + d) % nlst,
            )
            for d in range(1, nlst)
        ]
        for copy in r_copies:
            copy.start()
        for copy in r_copies:
            copy.wait_recv()
        s.row_scale[...] = 1.0 / added([s.row_sums[sweep, d] for d in range(nlst)])

        @pl.when(sweep < ITERS - 1)
        def _():
            wide = [
                jnp.broadcast_to(s.row_scale[m : m + 1, :], (16, LANES)).astype(BF16)
                for m in range(point_blocks)
            ]

            @pl.loop(0, list_blocks, unroll=4)
            def _(b):
                groups = []
                for q in range(LANES // 16):
                    rows = block(b * (LANES // 16) + q, 16)
                    groups.append(
                        added(
                            [
                                s.energy[rows, m * LANES : (m + 1) * LANES] * wide[m]
                                for m in range(point_blocks)
                            ]
                        )
                    )
                s.dense[pl.ds(b, 1), :] = lane_dense(jnp.concatenate(groups, axis=0))

        for copy in c_copies + r_copies:
            copy.wait_send()

    row_scale = s.row_scale[...]
    logs = jnp.log(row_scale)
    for m in range(point_blocks):
        row_log[place[m] : place[m] + 1, :] = logs[m : m + 1, :]

    for m in range(point_blocks):
        wide = column_of(row_scale[m : m + 1, :], LANES)
        values = points_of(m).astype(F32)
        for h in range(dp // LANES):
            lanes = slice(h * LANES, (h + 1) * LANES)
            s.scaled[m * LANES : (m + 1) * LANES, lanes] = (values[:, lanes] * wide).astype(BF16)

    tile = min(512, own)

    def chip_at(d):
        if chips == 4:
            return (chip // 2 + d // 2) % 2 * 2 + (chip + d) % 2
        return (chip + d) % chips

    def to_pair(d):
        return remote(
            s.pair_send.at[d],
            s.pair_recv.at[d],
            s.px_send.at[d],
            s.px_recv.at[d],
            "pts",
            pts + 1 - 2 * core,
        )

    def to_chip(d):
        return remote(
            s.chip_send.at[d],
            s.chip_recv.at[d],
            s.py_send.at[d],
            s.py_recv.at[d],
            "pts",
            chip_at(d) * 2 + core,
        )

    last = 2 * chips - 1

    @pl.loop(0, 2 * chips)
    def _(k):
        for_pair = (k == 0) | ((k % 2 == 1) & (k < last))
        turn = jnp.where(for_pair, (k + 1) // 2, jnp.where(k == last, chips - 1, k // 2 - 1))
        d = chips - 1 - turn
        owner = chip_at(d) * 2 + jnp.where(for_pair, 1 - core, core)

        @pl.loop(0, own // tile)
        def _(t):
            s.mine[block(t, tile), :] = jnp.dot(
                s.energy[block(owner * (own // tile) + t, tile), :],
                s.scaled[...],
                preferred_element_type=F32,
            )

        @pl.when(for_pair)
        def _():
            s.pair_send[d] = s.mine[...].astype(BF16)
            to_pair(d).start()

        @pl.when(jnp.logical_not(for_pair))
        def _():
            to_pair(d).wait_recv()
            both = s.mine[...] + s.pair_recv[d].astype(F32)

            @pl.when(d > 0)
            def _():
                s.chip_send[d] = both.astype(BF16)
                to_chip(d).start()

            @pl.when(d == 0)
            def _():
                s.mine[...] = both

    for d in range(1, chips):
        to_chip(d).wait_recv()
    for j in range(own // LANES):
        rows = slice(j * LANES, (j + 1) * LANES)
        sums = s.mine[rows, :]
        for d in range(1, chips):
            sums += s.chip_recv[d, rows, :].astype(F32)
        wide = column_of(s.dense[pl.ds(pts * (own // LANES) + j, 1), :], LANES)
        out[rows, :] = rms_norm(sums * jnp.concatenate([wide] * (dp // LANES), axis=1))
    for copy in pending:
        copy.wait_send()
    for d in range(chips):
        to_pair(d).wait_send()
    for d in range(1, chips):
        to_chip(d).wait_send()
    settle()


def in_line(points, nlst):
    return nlst == 4 and points % (2 * LANES) == 0


def on_device(npts, nlst, tower_out, projection, centroids):
    points, feats = tower_out.shape
    lists, dp = centroids.shape
    share = points // nlst
    own = lists // npts
    chips = npts // 2
    chunks = 2 if share % (2 * LANES) == 0 else 1
    vmem = pl.BlockSpec(memory_space=pltpu.VMEM)
    hbm = pl.BlockSpec(memory_space=pl.ANY)
    sem = pltpu.SemaphoreType.DMA
    scratch = dict(
        tower=pltpu.VMEM((points, feats), BF16),
        proj=pltpu.VMEM((feats, dp), BF16),
        unit=pltpu.VMEM((lists, dp), BF16),
        energy=pltpu.VMEM((lists, points), BF16),
        lane_sums=pltpu.VMEM((lists, LANES), F32),
        row_scale=pltpu.VMEM((points // LANES, LANES), F32),
        dense=pltpu.VMEM((lists // LANES, LANES), F32),
        col_sums=pltpu.VMEM((ITERS, npts, lists // LANES, LANES), BF16),
        row_sums=pltpu.VMEM((ITERS, nlst, points // LANES, LANES), F32),
        scaled=pltpu.VMEM((points, dp), BF16),
        pair_send=pltpu.VMEM((chips, own, dp), BF16),
        pair_recv=pltpu.VMEM((chips, own, dp), BF16),
        chip_send=pltpu.VMEM((chips, own, dp), BF16),
        chip_recv=pltpu.VMEM((chips, own, dp), BF16),
        mine=pltpu.VMEM((own, dp), F32),
        load=sem((3,)),
        c_send=sem((ITERS, npts)),
        c_recv=sem((ITERS, npts)),
        r_send=sem((ITERS, nlst)),
        r_recv=sem((ITERS, nlst)),
        px_send=sem((chips,)),
        px_recv=sem((chips,)),
        py_send=sem((chips,)),
        py_recv=sem((chips,)),
    )
    if in_line(points, nlst):
        scratch.update(line_scratch(points, lists, feats, dp))
    else:
        scratch.update(any_scratch(points, lists, feats, dp, npts, nlst, chunks))
    centers, row_log = pl.pallas_call(
        functools.partial(kernel, npts, nlst, chunks, tuple(scratch)),
        out_shape=(
            jax.ShapeDtypeStruct((own, dp), F32),
            jax.ShapeDtypeStruct((points // LANES, LANES), F32),
        ),
        in_specs=[hbm] * 3,
        out_specs=(vmem, vmem),
        scratch_shapes=list(scratch.values()),
        compiler_params=pltpu.CompilerParams(
            collective_id=0, has_side_effects=True, vmem_limit_bytes=60000000
        ),
    )(tower_out, projection, centroids)
    return centers, row_log.reshape(points)


def solution(mesh):
    return jax.shard_map(
        functools.partial(on_device, mesh.shape["pts"], mesh.shape["lst"]),
        mesh=mesh,
        in_specs=(P("pts", "lst"), P("lst", None), P("lst", None)),
        out_specs=(P(("lst", "pts"), None), P("pts")),
        check_vma=False,
    )
```

```python
import functools
import math
from types import SimpleNamespace

import jax
import jax.numpy as jnp
from jax import lax
from jax.experimental import pallas as pl
from jax.experimental.pallas import tpu as pltpu
from jax.sharding import PartitionSpec as P

ITERS = 3
temper = 0.05
LANES = 128
AHEAD = 2
MESH = pl.DeviceIdType.MESH
F32 = jnp.float32
BF16 = jnp.bfloat16


def rms_norm(values):
    return values * lax.rsqrt(jnp.mean(values * values, axis=-1, keepdims=True) + 1e-06)


def column_of(row, rows):
    return jnp.broadcast_to(row, (rows, LANES)).T


def added(terms):
    while len(terms) > 1:
        rest = terms[len(terms) // 2 * 2 :]
        terms = [terms[i] + terms[i + 1] for i in range(0, len(terms) - 1, 2)] + rest
    return terms[0]


def block(start, size):
    return pl.ds(pl.multiple_of(start * size, size), size)


def energy_block(s, gain, rows, cols, points):
    scores = lax.dot_general(
        s.unit[rows, :], points, (((1,), (1,)), ((), ())), preferred_element_type=F32
    )
    values = jnp.exp2(scores * gain)
    s.energy[rows, cols] = values.astype(BF16)
    width = values.shape[1] // LANES
    s.lane_sums[rows, :] += added([values[:, m * LANES : (m + 1) * LANES] for m in range(width)])


def unit_lists(s):
    lists = s.unit.shape[0]
    rows_each = min(256, lists)

    @pl.loop(0, lists // rows_each)
    def _(b):
        rows = block(b, rows_each)
        s.unit[rows, :] = rms_norm(s.unit[rows, :].astype(F32)).astype(BF16)
        s.lane_sums[rows, :] = jnp.zeros((rows_each, LANES), F32)


def line_gather(s, lst, gain, loads, arrive):
    points = s.tower.shape[0]
    lists = s.unit.shape[0]
    half = points // 2
    steps = half // LANES
    near = lst // 2
    far = 1 - near
    inner = (lst == 1) | (lst == 2)
    outer = jnp.logical_not(inner)
    inner_of_mine = 1 + near
    outer_of_mine = 3 * near
    other_inner = 2 - near

    def remote(src, dst, send_sem, recv_sem, target):
        return pltpu.make_async_remote_copy(
            src_ref=src,
            dst_ref=dst,
            send_sem=send_sem,
            recv_sem=recv_sem,
            device_id={"lst": target},
            device_id_type=MESH,
        )

    def feed(h, t):
        return remote(s.part.at[h, t], s.fed.at[h, t], s.f_send.at[h, t], s.f_recv.at[h, t], inner_of_mine)

    def cross(t):
        return remote(s.part.at[far, t], s.crossed.at[t], s.x_send.at[t], s.x_recv.at[t], other_inner)

    def back(u, h):
        return remote(
            s.normed.at[u, h], s.normed.at[u, h], s.b_send.at[u, h], s.n_recv.at[u, h], outer_of_mine
        )

    def across(u):
        return remote(
            s.normed.at[u, near], s.normed.at[u, near], s.a_send.at[u], s.n_recv.at[u, near], other_inner
        )

    def arrived(u, h):
        return remote(
            s.normed.at[u, h], s.normed.at[u, h], s.b_send.at[u, h], s.n_recv.at[u, h], other_inner
        )

    loads["proj"].wait()
    loads["tower"].wait()
    arrive()

    def partial(h, t):
        values = jnp.dot(
            s.tower[block(h * steps + t, LANES), :], s.proj[...], preferred_element_type=F32
        )

        @pl.when(outer)
        def _():
            s.part[h, t] = values.astype(BF16)
            feed(h, t).start()

        @pl.when(inner)
        def _():
            s.own[h, t] = values

    @pl.loop(0, steps + AHEAD)
    def _(t):
        @pl.when(t < steps)
        def _():
            partial(far, t)

        @pl.when(t >= AHEAD)
        def _():
            partial(near, t - AHEAD)

    e_rows = min(2048, lists)

    @pl.loop(0, steps + AHEAD + 1)
    def _(t):
        @pl.when(inner & (t < steps))
        def _():
            feed(far, t).wait_recv()
            s.part[far, t] = (s.own[far, t] + s.fed[far, t].astype(F32)).astype(BF16)
            cross(t).start()

        @pl.when(inner & (t >= AHEAD) & (t < steps + AHEAD))
        def _():
            u = t - AHEAD
            feed(near, u).wait_recv()
            cross(u).wait_recv()
            hidden = s.own[near, u] + s.fed[near, u].astype(F32) + s.crossed[u].astype(F32)
            s.normed[u, near] = rms_norm(hidden).astype(BF16)
            back(u, near).start()
            across(u).start()

        @pl.when(t == 1)
        def _():
            loads["cent"].wait()
            unit_lists(s)

        @pl.when(t > AHEAD)
        def _():
            u = t - AHEAD - 1

            @pl.when(inner)
            def _():
                arrived(u, far).wait_recv()
                back(u, far).start()

            @pl.when(outer)
            def _():
                arrived(u, near).wait_recv()
                arrived(u, far).wait_recv()

            @pl.loop(0, lists // e_rows)
            def _(b):
                rows = block(b, e_rows)
                pair = s.normed[u].reshape(2 * LANES, s.normed.shape[-1])
                energy_block(s, gain, rows, block(u, 2 * LANES), pair)

    def settle():
        @pl.loop(0, steps)
        def _(t):
            @pl.when(outer)
            def _():
                feed(far, t).wait_send()
                feed(near, t).wait_send()

            @pl.when(inner)
            def _():
                cross(t).wait_send()
                back(t, near).wait_send()
                back(t, far).wait_send()
                across(t).wait_send()

    def points_of(m):
        return s.normed[m // 2, m % 2]

    return settle, points_of, [h * steps + u for u in range(steps) for h in range(2)]


def line_scratch(points, lists, feats, dp):
    half = points // 2
    steps = half // LANES
    sem = pltpu.SemaphoreType.DMA
    return dict(
        own=pltpu.VMEM((2, steps, LANES, dp), F32),
        part=pltpu.VMEM((2, steps, LANES, dp), BF16),
        fed=pltpu.VMEM((2, steps, LANES, dp), BF16),
        crossed=pltpu.VMEM((steps, LANES, dp), BF16),
        normed=pltpu.VMEM((steps, 2, LANES, dp), BF16),
        f_send=sem((2, steps)),
        f_recv=sem((2, steps)),
        x_send=sem((steps,)),
        x_recv=sem((steps,)),
        b_send=sem((steps, 2)),
        a_send=sem((steps,)),
        n_recv=sem((steps, 2)),
    )


def any_gather(s, nlst, npts, lst, pts, send, chunks, gain, loads, arrive):
    points = s.tower.shape[0]
    lists = s.unit.shape[0]
    share = points // nlst
    feats = s.proj.shape[0]
    loads["proj"].wait()
    loads["tower"].wait()
    arrive()
    piece = feats // npts
    sliced = piece % 16 == 0
    piece_rows = block(pts, piece) if sliced else pl.ds(0, feats)
    p_copies = [
        send(
            s.proj.at[piece_rows],
            s.pfull.at[d, piece_rows],
            s.p_send.at[d],
            s.p_recv.at[d],
            "lst",
            (lst + d) % nlst,
        )
        for d in range(1, nlst)
    ]
    chunk = share // chunks
    t_copies = []
    for c in range(chunks):
        for d in range(1, nlst):
            z = (lst + d) % nlst
            t_copies.append(
                send(
                    s.tower.at[block(z * chunks + c, chunk)],
                    s.full.at[c, d],
                    s.t_send.at[c, d],
                    s.t_recv.at[c, d],
                    "lst",
                    z,
                )
            )
    loads["cent"].wait()
    unit_lists(s)

    for copy in p_copies:
        copy.wait_recv()
    if sliced:
        q_copies = [
            send(
                s.pfull.at[pl.ds(1, nlst - 1), piece_rows],
                s.pfull.at[pl.ds(1, nlst - 1), piece_rows],
                s.q_send.at[d],
                s.q_recv.at[d],
                "pts",
                (pts + d) % npts,
            )
            for d in range(1, npts)
        ]
        for copy in q_copies:
            copy.wait_recv()

    def hop(c, origin, left):
        side = 0 if left else 1
        return pltpu.make_async_remote_copy(
            src_ref=s.normed.at[c, origin],
            dst_ref=s.normed.at[c, origin],
            send_sem=s.n_send.at[side, c, origin],
            recv_sem=s.n_recv.at[c, origin],
            device_id={"lst": lst - 1 if left else lst + 1},
            device_id_type=MESH,
        )

    has_left = lst > 0
    has_right = lst < nlst - 1
    for c in range(chunks):
        hidden = jnp.dot(
            s.tower[block(lst * chunks + c, chunk), :], s.proj[...], preferred_element_type=F32
        )
        for d in range(1, nlst):
            t_copies[c * (nlst - 1) + d - 1].wait_recv()
            hidden += jnp.dot(s.full[c, d], s.pfull[d], preferred_element_type=F32)
        s.normed[c, lst] = rms_norm(hidden).astype(BF16)

        @pl.when(has_left)
        def _(c=c):
            hop(c, lst, True).start()

        @pl.when(has_right)
        def _(c=c):
            hop(c, lst, False).start()

    e_rows = min(1024, lists)
    step = min(256, chunk)
    per_share = share // step
    per_chunk = chunk // step

    def energy_of(c, origin):
        @pl.loop(0, lists // e_rows)
        def _(b):
            rows = block(b, e_rows)
            for k in range(per_chunk):
                cols = block(origin * per_share + c * per_chunk + k, step)
                energy_block(s, gain, rows, cols, s.normed[c, origin, k * step : (k + 1) * step, :])

    paired = jnp.minimum(lst, nlst - 1 - lst)
    for n in range(nlst):
        close = (n + 1) // 2
        away = n - paired
        in_pairs = lst - close if n % 2 else lst + close
        beyond = jnp.where(has_right & (lst < nlst - 1 - lst), lst + away, lst - away)
        origin = jnp.where(n <= 2 * paired, in_pairs, beyond) if n else lst
        for c in range(chunks):
            if n:
                hop(c, origin, True).wait_recv()

                @pl.when((origin < lst) & has_right)
                def _(c=c, origin=origin):
                    hop(c, origin, False).start()

                @pl.when((origin > lst) & has_left)
                def _(c=c, origin=origin):
                    hop(c, origin, True).start()

            energy_of(c, origin)

    def settle():
        for z in range(nlst):
            for c in range(chunks):

                @pl.when((z <= lst) & has_right)
                def _(c=c, z=z):
                    hop(c, z, False).wait_send()

                @pl.when((z >= lst) & has_left)
                def _(c=c, z=z):
                    hop(c, z, True).wait_send()

    def points_of(m):
        d, k = divmod(m * LANES, share)
        c, k = divmod(k, chunk)
        return s.normed[c, d, k : k + LANES, :]

    return settle, points_of, list(range(points // LANES))


def any_scratch(points, lists, feats, dp, npts, nlst, chunks):
    chunk = points // nlst // chunks
    sem = pltpu.SemaphoreType.DMA
    return dict(
        full=pltpu.VMEM((chunks, nlst, chunk, feats), BF16),
        pfull=pltpu.VMEM((nlst, feats, dp), BF16),
        normed=pltpu.VMEM((chunks, nlst, chunk, dp), BF16),
        t_send=sem((chunks, nlst)),
        t_recv=sem((chunks, nlst)),
        p_send=sem((nlst,)),
        p_recv=sem((nlst,)),
        q_send=sem((npts,)),
        q_recv=sem((npts,)),
        n_send=sem((2, chunks, nlst)),
        n_recv=sem((chunks, nlst)),
    )


def kernel(npts, nlst, chunks, names, tower, proj, cent, out, row_log, *scratch):
    s = SimpleNamespace(**dict(zip(names, scratch)))
    pts = lax.axis_index("pts")
    lst = lax.axis_index("lst")
    lists, dp = s.unit.shape
    points = s.tower.shape[0]
    own = lists // npts
    chips = npts // 2
    core = pts % 2
    chip = pts // 2
    balance = (points * npts) / (lists * nlst)
    list_blocks = lists // LANES
    point_blocks = points // LANES

    loads = {
        "proj": pltpu.make_async_copy(proj, s.proj, s.load.at[0]),
        "tower": pltpu.make_async_copy(tower, s.tower, s.load.at[1]),
        "cent": pltpu.make_async_copy(cent, s.unit, s.load.at[2]),
    }
    for copy in loads.values():
        copy.start()

    barrier = pltpu.get_barrier_semaphore()
    for d in range(1, nlst):
        pl.semaphore_signal(
            barrier, inc=1, device_id={"lst": (lst + d) % nlst}, device_id_type=MESH
        )
    for d in range(1, npts):
        pl.semaphore_signal(
            barrier, inc=1, device_id={"pts": (pts + d) % npts}, device_id_type=MESH
        )

    def arrive():
        pl.semaphore_wait(barrier, nlst + npts - 2)

    pending = []

    def remote(src, dst, send_sem, recv_sem, axis, target):
        return pltpu.make_async_remote_copy(
            src_ref=src,
            dst_ref=dst,
            send_sem=send_sem,
            recv_sem=recv_sem,
            device_id={axis: target},
            device_id_type=MESH,
        )

    def send(*what):
        copy = remote(*what)
        copy.start()
        pending.append(copy)
        return copy

    gain = 1.0 / (math.log(2.0) * dp * temper)
    if in_line(points, nlst):
        settle, points_of, place = line_gather(s, lst, gain, loads, arrive)
    else:
        settle, points_of, place = any_gather(
            s, nlst, npts, lst, pts, send, chunks, gain, loads, arrive
        )

    def lane_dense(sums):
        return jnp.sum(sums.T, axis=0, keepdims=True)

    @pl.loop(0, list_blocks, unroll=8)
    def _(b):
        s.dense[pl.ds(b, 1), :] = lane_dense(s.lane_sums[block(b, LANES), :])

    @pl.loop(0, ITERS)
    def _(sweep):
        s.col_sums[sweep, 0] = s.dense[...].astype(BF16)
        c_copies = [
            remote(
                s.col_sums.at[sweep, 0],
                s.col_sums.at[sweep, d],
                s.c_send.at[sweep, d],
                s.c_recv.at[sweep, d],
                "pts",
                (pts + d) % npts,
            )
            for d in range(1, npts)
        ]
        for copy in c_copies:
            copy.start()
        for copy in c_copies:
            copy.wait_recv()
        total = added([s.col_sums[sweep, d].astype(F32) for d in range(npts)])
        s.dense[...] = balance / total

        depth = min(512, lists)
        acc = jnp.zeros((16, points), F32)
        for b in range(lists // depth):
            scales = [
                jnp.broadcast_to(s.dense[k : k + 1, :], (16, LANES)).astype(BF16)
                for k in range(b * (depth // LANES), (b + 1) * (depth // LANES))
            ]
            acc += jnp.dot(
                jnp.concatenate(scales, axis=1),
                s.energy[b * depth : (b + 1) * depth, :],
                preferred_element_type=F32,
            )
        s.row_sums[sweep, 0] = jnp.concatenate(
            [acc[0:1, m * LANES : (m + 1) * LANES] for m in range(point_blocks)], axis=0
        )
        r_copies = [
            remote(
                s.row_sums.at[sweep, 0],
                s.row_sums.at[sweep, d],
                s.r_send.at[sweep, d],
                s.r_recv.at[sweep, d],
                "lst",
                (lst + d) % nlst,
            )
            for d in range(1, nlst)
        ]
        for copy in r_copies:
            copy.start()
        for copy in r_copies:
            copy.wait_recv()
        s.row_scale[...] = 1.0 / added([s.row_sums[sweep, d] for d in range(nlst)])

        @pl.when(sweep < ITERS - 1)
        def _():
            wide = [
                jnp.broadcast_to(s.row_scale[m : m + 1, :], (16, LANES)).astype(BF16)
                for m in range(point_blocks)
            ]

            @pl.loop(0, list_blocks, unroll=8)
            def _(b):
                groups = []
                for q in range(LANES // 16):
                    rows = block(b * (LANES // 16) + q, 16)
                    groups.append(
                        added(
                            [
                                s.energy[rows, m * LANES : (m + 1) * LANES] * wide[m]
                                for m in range(point_blocks)
                            ]
                        )
                    )
                s.dense[pl.ds(b, 1), :] = lane_dense(jnp.concatenate(groups, axis=0).astype(F32))

        for copy in c_copies + r_copies:
            copy.wait_send()

    row_scale = s.row_scale[...]
    logs = jnp.log(row_scale)
    for m in range(point_blocks):
        row_log[place[m] : place[m] + 1, :] = logs[m : m + 1, :]

    for m in range(point_blocks):
        wide = column_of(row_scale[m : m + 1, :], LANES)
        values = points_of(m).astype(F32)
        for h in range(dp // LANES):
            lanes = slice(h * LANES, (h + 1) * LANES)
            s.scaled[m * LANES : (m + 1) * LANES, lanes] = (values[:, lanes] * wide).astype(BF16)

    tile = min(512, own)

    def chip_at(d):
        if chips == 4:
            return (chip // 2 + d // 2) % 2 * 2 + (chip + d) % 2
        return (chip + d) % chips

    def to_pair(d):
        return remote(
            s.pair_send.at[d],
            s.pair_recv.at[d],
            s.px_send.at[d],
            s.px_recv.at[d],
            "pts",
            pts + 1 - 2 * core,
        )

    def to_chip(d):
        return remote(
            s.chip_send.at[d],
            s.chip_recv.at[d],
            s.py_send.at[d],
            s.py_recv.at[d],
            "pts",
            chip_at(d) * 2 + core,
        )

    last = 2 * chips - 1

    @pl.loop(0, 2 * chips)
    def _(k):
        for_pair = (k == 0) | ((k % 2 == 1) & (k < last))
        turn = jnp.where(for_pair, (k + 1) // 2, jnp.where(k == last, chips - 1, k // 2 - 1))
        d = chips - 1 - turn
        owner = chip_at(d) * 2 + jnp.where(for_pair, 1 - core, core)

        @pl.loop(0, own // tile)
        def _(t):
            s.mine[block(t, tile), :] = jnp.dot(
                s.energy[block(owner * (own // tile) + t, tile), :],
                s.scaled[...],
                preferred_element_type=F32,
            )

        @pl.when(for_pair)
        def _():
            s.pair_send[d] = s.mine[...].astype(BF16)
            to_pair(d).start()

        @pl.when(jnp.logical_not(for_pair))
        def _():
            to_pair(d).wait_recv()
            both = s.mine[...] + s.pair_recv[d].astype(F32)

            @pl.when(d > 0)
            def _():
                s.chip_send[d] = both.astype(BF16)
                to_chip(d).start()

            @pl.when(d == 0)
            def _():
                s.mine[...] = both

    for d in range(1, chips):
        to_chip(d).wait_recv()
    for j in range(own // LANES):
        rows = slice(j * LANES, (j + 1) * LANES)
        sums = s.mine[rows, :]
        for d in range(1, chips):
            sums += s.chip_recv[d, rows, :].astype(F32)
        wide = column_of(s.dense[pl.ds(pts * (own // LANES) + j, 1), :], LANES)
        out[rows, :] = rms_norm(sums * jnp.concatenate([wide] * (dp // LANES), axis=1))
    for copy in pending:
        copy.wait_send()
    for d in range(chips):
        to_pair(d).wait_send()
    for d in range(1, chips):
        to_chip(d).wait_send()
    settle()


def in_line(points, nlst):
    return nlst == 4 and points % (2 * LANES) == 0


def on_device(npts, nlst, tower_out, projection, centroids):
    points, feats = tower_out.shape
    lists, dp = centroids.shape
    share = points // nlst
    own = lists // npts
    chips = npts // 2
    chunks = 2 if share % (2 * LANES) == 0 else 1
    vmem = pl.BlockSpec(memory_space=pltpu.VMEM)
    hbm = pl.BlockSpec(memory_space=pl.ANY)
    sem = pltpu.SemaphoreType.DMA
    scratch = dict(
        tower=pltpu.VMEM((points, feats), BF16),
        proj=pltpu.VMEM((feats, dp), BF16),
        unit=pltpu.VMEM((lists, dp), BF16),
        energy=pltpu.VMEM((lists, points), BF16),
        lane_sums=pltpu.VMEM((lists, LANES), F32),
        row_scale=pltpu.VMEM((points // LANES, LANES), F32),
        dense=pltpu.VMEM((lists // LANES, LANES), F32),
        col_sums=pltpu.VMEM((ITERS, npts, lists // LANES, LANES), BF16),
        row_sums=pltpu.VMEM((ITERS, nlst, points // LANES, LANES), F32),
        scaled=pltpu.VMEM((points, dp), BF16),
        pair_send=pltpu.VMEM((chips, own, dp), BF16),
        pair_recv=pltpu.VMEM((chips, own, dp), BF16),
        chip_send=pltpu.VMEM((chips, own, dp), BF16),
        chip_recv=pltpu.VMEM((chips, own, dp), BF16),
        mine=pltpu.VMEM((own, dp), F32),
        load=sem((3,)),
        c_send=sem((ITERS, npts)),
        c_recv=sem((ITERS, npts)),
        r_send=sem((ITERS, nlst)),
        r_recv=sem((ITERS, nlst)),
        px_send=sem((chips,)),
        px_recv=sem((chips,)),
        py_send=sem((chips,)),
        py_recv=sem((chips,)),
    )
    if in_line(points, nlst):
        scratch.update(line_scratch(points, lists, feats, dp))
    else:
        scratch.update(any_scratch(points, lists, feats, dp, npts, nlst, chunks))
    centers, row_log = pl.pallas_call(
        functools.partial(kernel, npts, nlst, chunks, tuple(scratch)),
        out_shape=(
            jax.ShapeDtypeStruct((own, dp), F32),
            jax.ShapeDtypeStruct((points // LANES, LANES), F32),
        ),
        in_specs=[hbm] * 3,
        out_specs=(vmem, vmem),
        scratch_shapes=list(scratch.values()),
        compiler_params=pltpu.CompilerParams(
            collective_id=0, has_side_effects=True, vmem_limit_bytes=60000000
        ),
    )(tower_out, projection, centroids)
    return centers, row_log.reshape(points)


def solution(mesh):
    return jax.shard_map(
        functools.partial(on_device, mesh.shape["pts"], mesh.shape["lst"]),
        mesh=mesh,
        in_specs=(P("pts", "lst"), P("lst", None), P("lst", None)),
        out_specs=(P(("lst", "pts"), None), P("pts")),
        check_vma=False,
    )
```

```python
import functools
import math
from types import SimpleNamespace

import jax
import jax.numpy as jnp
from jax import lax
from jax.experimental import pallas as pl
from jax.experimental.pallas import tpu as pltpu
from jax.sharding import PartitionSpec as P

ITERS = 3
temper = 0.05
LANES = 128
AHEAD = 2
MESH = pl.DeviceIdType.MESH
F32 = jnp.float32
BF16 = jnp.bfloat16


def rms_norm(values):
    return values * lax.rsqrt(jnp.mean(values * values, axis=-1, keepdims=True) + 1e-06)


def column_of(row, rows):
    return jnp.broadcast_to(row, (rows, LANES)).T


def added(terms):
    while len(terms) > 1:
        rest = terms[len(terms) // 2 * 2 :]
        terms = [terms[i] + terms[i + 1] for i in range(0, len(terms) - 1, 2)] + rest
    return terms[0]


def block(start, size):
    return pl.ds(pl.multiple_of(start * size, size), size)


def energy_block(s, gain, rows, cols, points):
    scores = lax.dot_general(
        s.unit[rows, :], points, (((1,), (1,)), ((), ())), preferred_element_type=F32
    )
    values = jnp.exp2(scores * gain)
    s.energy[rows, cols] = values.astype(BF16)
    width = values.shape[1] // LANES
    s.lane_sums[rows, :] += added([values[:, m * LANES : (m + 1) * LANES] for m in range(width)])


def unit_lists(s):
    lists = s.unit.shape[0]
    rows_each = min(256, lists)

    @pl.loop(0, lists // rows_each)
    def _(b):
        rows = block(b, rows_each)
        s.unit[rows, :] = rms_norm(s.unit[rows, :].astype(F32)).astype(BF16)
        s.lane_sums[rows, :] = jnp.zeros((rows_each, LANES), F32)


def line_gather(s, lst, gain, loads, arrive):
    points = s.tower.shape[0]
    lists = s.unit.shape[0]
    half = points // 2
    steps = half // LANES
    near = lst // 2
    far = 1 - near
    inner = (lst == 1) | (lst == 2)
    outer = jnp.logical_not(inner)
    inner_of_mine = 1 + near
    outer_of_mine = 3 * near
    other_inner = 2 - near

    def remote(src, dst, send_sem, recv_sem, target):
        return pltpu.make_async_remote_copy(
            src_ref=src,
            dst_ref=dst,
            send_sem=send_sem,
            recv_sem=recv_sem,
            device_id={"lst": target},
            device_id_type=MESH,
        )

    def feed(h, t):
        return remote(s.part.at[h, t], s.fed.at[h, t], s.f_send.at[h, t], s.f_recv.at[h, t], inner_of_mine)

    def cross(t):
        return remote(s.part.at[far, t], s.crossed.at[t], s.x_send.at[t], s.x_recv.at[t], other_inner)

    def back(u, h):
        return remote(
            s.normed.at[u, h], s.normed.at[u, h], s.b_send.at[u, h], s.n_recv.at[u, h], outer_of_mine
        )

    def across(u):
        return remote(
            s.normed.at[u, near], s.normed.at[u, near], s.a_send.at[u], s.n_recv.at[u, near], other_inner
        )

    def arrived(u, h):
        return remote(
            s.normed.at[u, h], s.normed.at[u, h], s.b_send.at[u, h], s.n_recv.at[u, h], other_inner
        )

    loads["proj"].wait()
    loads["tower"].wait()
    arrive()

    def partial(h, t):
        values = jnp.dot(
            s.tower[block(h * steps + t, LANES), :], s.proj[...], preferred_element_type=F32
        )

        @pl.when(outer)
        def _():
            s.part[h, t] = values.astype(BF16)
            feed(h, t).start()

        @pl.when(inner)
        def _():
            s.own[h, t] = values

    @pl.loop(0, steps + AHEAD)
    def _(t):
        @pl.when(t < steps)
        def _():
            partial(far, t)

        @pl.when(t >= AHEAD)
        def _():
            partial(near, t - AHEAD)

    e_rows = min(4096, lists)

    @pl.loop(0, steps + AHEAD + 1)
    def _(t):
        @pl.when(inner & (t < steps))
        def _():
            feed(far, t).wait_recv()
            s.part[far, t] = (s.own[far, t] + s.fed[far, t].astype(F32)).astype(BF16)
            cross(t).start()

        @pl.when(inner & (t >= AHEAD) & (t < steps + AHEAD))
        def _():
            u = t - AHEAD
            feed(near, u).wait_recv()
            cross(u).wait_recv()
            hidden = s.own[near, u] + s.fed[near, u].astype(F32) + s.crossed[u].astype(F32)
            s.normed[u, near] = rms_norm(hidden).astype(BF16)
            back(u, near).start()
            across(u).start()

        @pl.when(t == 1)
        def _():
            loads["cent"].wait()
            unit_lists(s)

        @pl.when(t > AHEAD)
        def _():
            u = t - AHEAD - 1

            @pl.when(inner)
            def _():
                arrived(u, far).wait_recv()
                back(u, far).start()

            @pl.when(outer)
            def _():
                arrived(u, near).wait_recv()
                arrived(u, far).wait_recv()

            @pl.loop(0, lists // e_rows)
            def _(b):
                rows = block(b, e_rows)
                pair = s.normed[u].reshape(2 * LANES, s.normed.shape[-1])
                energy_block(s, gain, rows, block(u, 2 * LANES), pair)

    def settle():
        @pl.loop(0, steps)
        def _(t):
            @pl.when(outer)
            def _():
                feed(far, t).wait_send()
                feed(near, t).wait_send()

            @pl.when(inner)
            def _():
                cross(t).wait_send()
                back(t, near).wait_send()
                back(t, far).wait_send()
                across(t).wait_send()

    def points_of(m):
        return s.normed[m // 2, m % 2]

    return settle, points_of, [h * steps + u for u in range(steps) for h in range(2)]


def line_scratch(points, lists, feats, dp):
    half = points // 2
    steps = half // LANES
    sem = pltpu.SemaphoreType.DMA
    return dict(
        own=pltpu.VMEM((2, steps, LANES, dp), F32),
        part=pltpu.VMEM((2, steps, LANES, dp), BF16),
        fed=pltpu.VMEM((2, steps, LANES, dp), BF16),
        crossed=pltpu.VMEM((steps, LANES, dp), BF16),
        normed=pltpu.VMEM((steps, 2, LANES, dp), BF16),
        f_send=sem((2, steps)),
        f_recv=sem((2, steps)),
        x_send=sem((steps,)),
        x_recv=sem((steps,)),
        b_send=sem((steps, 2)),
        a_send=sem((steps,)),
        n_recv=sem((steps, 2)),
    )


def any_gather(s, nlst, npts, lst, pts, send, chunks, gain, loads, arrive):
    points = s.tower.shape[0]
    lists = s.unit.shape[0]
    share = points // nlst
    feats = s.proj.shape[0]
    loads["proj"].wait()
    loads["tower"].wait()
    arrive()
    piece = feats // npts
    sliced = piece % 16 == 0
    piece_rows = block(pts, piece) if sliced else pl.ds(0, feats)
    p_copies = [
        send(
            s.proj.at[piece_rows],
            s.pfull.at[d, piece_rows],
            s.p_send.at[d],
            s.p_recv.at[d],
            "lst",
            (lst + d) % nlst,
        )
        for d in range(1, nlst)
    ]
    chunk = share // chunks
    t_copies = []
    for c in range(chunks):
        for d in range(1, nlst):
            z = (lst + d) % nlst
            t_copies.append(
                send(
                    s.tower.at[block(z * chunks + c, chunk)],
                    s.full.at[c, d],
                    s.t_send.at[c, d],
                    s.t_recv.at[c, d],
                    "lst",
                    z,
                )
            )
    loads["cent"].wait()
    unit_lists(s)

    for copy in p_copies:
        copy.wait_recv()
    if sliced:
        q_copies = [
            send(
                s.pfull.at[pl.ds(1, nlst - 1), piece_rows],
                s.pfull.at[pl.ds(1, nlst - 1), piece_rows],
                s.q_send.at[d],
                s.q_recv.at[d],
                "pts",
                (pts + d) % npts,
            )
            for d in range(1, npts)
        ]
        for copy in q_copies:
            copy.wait_recv()

    def hop(c, origin, left):
        side = 0 if left else 1
        return pltpu.make_async_remote_copy(
            src_ref=s.normed.at[c, origin],
            dst_ref=s.normed.at[c, origin],
            send_sem=s.n_send.at[side, c, origin],
            recv_sem=s.n_recv.at[c, origin],
            device_id={"lst": lst - 1 if left else lst + 1},
            device_id_type=MESH,
        )

    has_left = lst > 0
    has_right = lst < nlst - 1
    for c in range(chunks):
        hidden = jnp.dot(
            s.tower[block(lst * chunks + c, chunk), :], s.proj[...], preferred_element_type=F32
        )
        for d in range(1, nlst):
            t_copies[c * (nlst - 1) + d - 1].wait_recv()
            hidden += jnp.dot(s.full[c, d], s.pfull[d], preferred_element_type=F32)
        s.normed[c, lst] = rms_norm(hidden).astype(BF16)

        @pl.when(has_left)
        def _(c=c):
            hop(c, lst, True).start()

        @pl.when(has_right)
        def _(c=c):
            hop(c, lst, False).start()

    e_rows = min(1024, lists)
    step = min(256, chunk)
    per_share = share // step
    per_chunk = chunk // step

    def energy_of(c, origin):
        @pl.loop(0, lists // e_rows)
        def _(b):
            rows = block(b, e_rows)
            for k in range(per_chunk):
                cols = block(origin * per_share + c * per_chunk + k, step)
                energy_block(s, gain, rows, cols, s.normed[c, origin, k * step : (k + 1) * step, :])

    paired = jnp.minimum(lst, nlst - 1 - lst)
    for n in range(nlst):
        close = (n + 1) // 2
        away = n - paired
        in_pairs = lst - close if n % 2 else lst + close
        beyond = jnp.where(has_right & (lst < nlst - 1 - lst), lst + away, lst - away)
        origin = jnp.where(n <= 2 * paired, in_pairs, beyond) if n else lst
        for c in range(chunks):
            if n:
                hop(c, origin, True).wait_recv()

                @pl.when((origin < lst) & has_right)
                def _(c=c, origin=origin):
                    hop(c, origin, False).start()

                @pl.when((origin > lst) & has_left)
                def _(c=c, origin=origin):
                    hop(c, origin, True).start()

            energy_of(c, origin)

    def settle():
        for z in range(nlst):
            for c in range(chunks):

                @pl.when((z <= lst) & has_right)
                def _(c=c, z=z):
                    hop(c, z, False).wait_send()

                @pl.when((z >= lst) & has_left)
                def _(c=c, z=z):
                    hop(c, z, True).wait_send()

    def points_of(m):
        d, k = divmod(m * LANES, share)
        c, k = divmod(k, chunk)
        return s.normed[c, d, k : k + LANES, :]

    return settle, points_of, list(range(points // LANES))


def any_scratch(points, lists, feats, dp, npts, nlst, chunks):
    chunk = points // nlst // chunks
    sem = pltpu.SemaphoreType.DMA
    return dict(
        full=pltpu.VMEM((chunks, nlst, chunk, feats), BF16),
        pfull=pltpu.VMEM((nlst, feats, dp), BF16),
        normed=pltpu.VMEM((chunks, nlst, chunk, dp), BF16),
        t_send=sem((chunks, nlst)),
        t_recv=sem((chunks, nlst)),
        p_send=sem((nlst,)),
        p_recv=sem((nlst,)),
        q_send=sem((npts,)),
        q_recv=sem((npts,)),
        n_send=sem((2, chunks, nlst)),
        n_recv=sem((chunks, nlst)),
    )


def kernel(npts, nlst, chunks, names, tower, proj, cent, out, row_log, *scratch):
    s = SimpleNamespace(**dict(zip(names, scratch)))
    pts = lax.axis_index("pts")
    lst = lax.axis_index("lst")
    lists, dp = s.unit.shape
    points = s.tower.shape[0]
    own = lists // npts
    chips = npts // 2
    core = pts % 2
    chip = pts // 2
    balance = (points * npts) / (lists * nlst)
    list_blocks = lists // LANES
    point_blocks = points // LANES

    loads = {
        "proj": pltpu.make_async_copy(proj, s.proj, s.load.at[0]),
        "tower": pltpu.make_async_copy(tower, s.tower, s.load.at[1]),
        "cent": pltpu.make_async_copy(cent, s.unit, s.load.at[2]),
    }
    for copy in loads.values():
        copy.start()

    barrier = pltpu.get_barrier_semaphore()
    for d in range(1, nlst):
        pl.semaphore_signal(
            barrier, inc=1, device_id={"lst": (lst + d) % nlst}, device_id_type=MESH
        )
    for d in range(1, npts):
        pl.semaphore_signal(
            barrier, inc=1, device_id={"pts": (pts + d) % npts}, device_id_type=MESH
        )

    def arrive():
        pl.semaphore_wait(barrier, nlst + npts - 2)

    pending = []

    def remote(src, dst, send_sem, recv_sem, axis, target):
        return pltpu.make_async_remote_copy(
            src_ref=src,
            dst_ref=dst,
            send_sem=send_sem,
            recv_sem=recv_sem,
            device_id={axis: target},
            device_id_type=MESH,
        )

    def send(*what):
        copy = remote(*what)
        copy.start()
        pending.append(copy)
        return copy

    gain = 1.0 / (math.log(2.0) * dp * temper)
    if in_line(points, nlst):
        settle, points_of, place = line_gather(s, lst, gain, loads, arrive)
    else:
        settle, points_of, place = any_gather(
            s, nlst, npts, lst, pts, send, chunks, gain, loads, arrive
        )

    def lane_dense(sums):
        return jnp.sum(sums.T, axis=0, keepdims=True)

    @pl.loop(0, list_blocks, unroll=min(16, list_blocks))
    def _(b):
        s.dense[pl.ds(b, 1), :] = lane_dense(s.lane_sums[block(b, LANES), :])

    @pl.loop(0, ITERS)
    def _(sweep):
        s.col_sums[sweep, 0] = s.dense[...].astype(BF16)
        c_copies = [
            remote(
                s.col_sums.at[sweep, 0],
                s.col_sums.at[sweep, d],
                s.c_send.at[sweep, d],
                s.c_recv.at[sweep, d],
                "pts",
                (pts + d) % npts,
            )
            for d in range(1, npts)
        ]
        for copy in c_copies:
            copy.start()
        for copy in c_copies:
            copy.wait_recv()
        total = added([s.col_sums[sweep, d].astype(F32) for d in range(npts)])
        s.dense[...] = balance / total

        depth = min(512, lists)
        acc = jnp.zeros((16, points), F32)
        for b in range(lists // depth):
            scales = [
                jnp.broadcast_to(s.dense[k : k + 1, :], (16, LANES)).astype(BF16)
                for k in range(b * (depth // LANES), (b + 1) * (depth // LANES))
            ]
            acc += jnp.dot(
                jnp.concatenate(scales, axis=1),
                s.energy[b * depth : (b + 1) * depth, :],
                preferred_element_type=F32,
            )
        s.row_sums[sweep, 0] = jnp.concatenate(
            [acc[0:1, m * LANES : (m + 1) * LANES] for m in range(point_blocks)], axis=0
        )
        r_copies = [
            remote(
                s.row_sums.at[sweep, 0],
                s.row_sums.at[sweep, d],
                s.r_send.at[sweep, d],
                s.r_recv.at[sweep, d],
                "lst",
                (lst + d) % nlst,
            )
            for d in range(1, nlst)
        ]
        for copy in r_copies:
            copy.start()
        for copy in r_copies:
            copy.wait_recv()
        s.row_scale[...] = 1.0 / added([s.row_sums[sweep, d] for d in range(nlst)])

        @pl.when(sweep < ITERS - 1)
        def _():
            wide = [
                jnp.broadcast_to(s.row_scale[m : m + 1, :], (16, LANES)).astype(BF16)
                for m in range(point_blocks)
            ]

            @pl.loop(0, list_blocks, unroll=min(16, list_blocks))
            def _(b):
                groups = []
                for q in range(LANES // 16):
                    rows = block(b * (LANES // 16) + q, 16)
                    groups.append(
                        added(
                            [
                                s.energy[rows, m * LANES : (m + 1) * LANES] * wide[m]
                                for m in range(point_blocks)
                            ]
                        )
                    )
                s.dense[pl.ds(b, 1), :] = lane_dense(jnp.concatenate(groups, axis=0).astype(F32))

        for copy in c_copies + r_copies:
            copy.wait_send()

    row_scale = s.row_scale[...]
    logs = jnp.log(row_scale)
    for m in range(point_blocks):
        row_log[place[m] : place[m] + 1, :] = logs[m : m + 1, :]

    for m in range(point_blocks):
        wide = column_of(row_scale[m : m + 1, :], LANES)
        values = points_of(m).astype(F32)
        for h in range(dp // LANES):
            lanes = slice(h * LANES, (h + 1) * LANES)
            s.scaled[m * LANES : (m + 1) * LANES, lanes] = (values[:, lanes] * wide).astype(BF16)

    tile = min(512, own)

    def chip_at(d):
        if chips == 4:
            return (chip // 2 + d // 2) % 2 * 2 + (chip + d) % 2
        return (chip + d) % chips

    def to_pair(d):
        return remote(
            s.pair_send.at[d],
            s.pair_recv.at[d],
            s.px_send.at[d],
            s.px_recv.at[d],
            "pts",
            pts + 1 - 2 * core,
        )

    def to_chip(d):
        return remote(
            s.chip_send.at[d],
            s.chip_recv.at[d],
            s.py_send.at[d],
            s.py_recv.at[d],
            "pts",
            chip_at(d) * 2 + core,
        )

    last = 2 * chips - 1

    @pl.loop(0, 2 * chips)
    def _(k):
        for_pair = (k == 0) | ((k % 2 == 1) & (k < last))
        turn = jnp.where(for_pair, (k + 1) // 2, jnp.where(k == last, chips - 1, k // 2 - 1))
        d = chips - 1 - turn
        owner = chip_at(d) * 2 + jnp.where(for_pair, 1 - core, core)

        @pl.loop(0, own // tile)
        def _(t):
            s.mine[block(t, tile), :] = jnp.dot(
                s.energy[block(owner * (own // tile) + t, tile), :],
                s.scaled[...],
                preferred_element_type=F32,
            )

        @pl.when(for_pair)
        def _():
            s.pair_send[d] = s.mine[...].astype(BF16)
            to_pair(d).start()

        @pl.when(jnp.logical_not(for_pair))
        def _():
            to_pair(d).wait_recv()
            both = s.mine[...] + s.pair_recv[d].astype(F32)

            @pl.when(d > 0)
            def _():
                s.chip_send[d] = both.astype(BF16)
                to_chip(d).start()

            @pl.when(d == 0)
            def _():
                s.mine[...] = both

    for d in range(1, chips):
        to_chip(d).wait_recv()
    for j in range(own // LANES):
        rows = slice(j * LANES, (j + 1) * LANES)
        sums = s.mine[rows, :]
        for d in range(1, chips):
            sums += s.chip_recv[d, rows, :].astype(F32)
        wide = column_of(s.dense[pl.ds(pts * (own // LANES) + j, 1), :], LANES)
        out[rows, :] = rms_norm(sums * jnp.concatenate([wide] * (dp // LANES), axis=1))
    for copy in pending:
        copy.wait_send()
    for d in range(chips):
        to_pair(d).wait_send()
    for d in range(1, chips):
        to_chip(d).wait_send()
    settle()


def in_line(points, nlst):
    return nlst == 4 and points % (2 * LANES) == 0


def on_device(npts, nlst, tower_out, projection, centroids):
    points, feats = tower_out.shape
    lists, dp = centroids.shape
    share = points // nlst
    own = lists // npts
    chips = npts // 2
    chunks = 2 if share % (2 * LANES) == 0 else 1
    vmem = pl.BlockSpec(memory_space=pltpu.VMEM)
    hbm = pl.BlockSpec(memory_space=pl.ANY)
    sem = pltpu.SemaphoreType.DMA
    scratch = dict(
        tower=pltpu.VMEM((points, feats), BF16),
        proj=pltpu.VMEM((feats, dp), BF16),
        unit=pltpu.VMEM((lists, dp), BF16),
        energy=pltpu.VMEM((lists, points), BF16),
        lane_sums=pltpu.VMEM((lists, LANES), F32),
        row_scale=pltpu.VMEM((points // LANES, LANES), F32),
        dense=pltpu.VMEM((lists // LANES, LANES), F32),
        col_sums=pltpu.VMEM((ITERS, npts, lists // LANES, LANES), BF16),
        row_sums=pltpu.VMEM((ITERS, nlst, points // LANES, LANES), F32),
        scaled=pltpu.VMEM((points, dp), BF16),
        pair_send=pltpu.VMEM((chips, own, dp), BF16),
        pair_recv=pltpu.VMEM((chips, own, dp), BF16),
        chip_send=pltpu.VMEM((chips, own, dp), BF16),
        chip_recv=pltpu.VMEM((chips, own, dp), BF16),
        mine=pltpu.VMEM((own, dp), F32),
        load=sem((3,)),
        c_send=sem((ITERS, npts)),
        c_recv=sem((ITERS, npts)),
        r_send=sem((ITERS, nlst)),
        r_recv=sem((ITERS, nlst)),
        px_send=sem((chips,)),
        px_recv=sem((chips,)),
        py_send=sem((chips,)),
        py_recv=sem((chips,)),
    )
    if in_line(points, nlst):
        scratch.update(line_scratch(points, lists, feats, dp))
    else:
        scratch.update(any_scratch(points, lists, feats, dp, npts, nlst, chunks))
    centers, row_log = pl.pallas_call(
        functools.partial(kernel, npts, nlst, chunks, tuple(scratch)),
        out_shape=(
            jax.ShapeDtypeStruct((own, dp), F32),
            jax.ShapeDtypeStruct((points // LANES, LANES), F32),
        ),
        in_specs=[hbm] * 3,
        out_specs=(vmem, vmem),
        scratch_shapes=list(scratch.values()),
        compiler_params=pltpu.CompilerParams(
            collective_id=0, has_side_effects=True, vmem_limit_bytes=60000000
        ),
    )(tower_out, projection, centroids)
    return centers, row_log.reshape(points)


def solution(mesh):
    return jax.shard_map(
        functools.partial(on_device, mesh.shape["pts"], mesh.shape["lst"]),
        mesh=mesh,
        in_specs=(P("pts", "lst"), P("lst", None), P("lst", None)),
        out_specs=(P(("lst", "pts"), None), P("pts")),
        check_vma=False,
    )
```
